32 devices in a mesh: horiz: 8 (over z, core), vert: 4 (over y, x).
Axes of the slice: x: 2, y: 2, z: 4, core: 2. Of those that a mesh axis runs over, the one named last changes fastest.
Arguments:
- chi: float32 [128, 131072], P('vert', 'horiz'), may hold values from -6 to 6
- bg_std: float32 [128, 131072], P('vert', 'horiz'), may hold values from 0.3 to 3
- vert_root: float32 [128, 128], replicated, may hold values from -0.5 to 0.5
- obs_blocks: bfloat16 [128, 128, 2, 128, 128], P('horiz', 'vert'), may hold values from -0.03125 to 0.03125
- block_cols: int32 [128, 128, 2], P('horiz', 'vert'), may hold values from 0 to 1023, as said below
- departures: float32 [16384], P(('horiz', 'vert')), may hold values from -6 to 6
- obs_std: float32 [16384], P(('horiz', 'vert')), may hold values from 0.5 to 2
- obs_target: int32 [16384], P(('horiz', 'vert')), may hold values from 0 to 16383, as said below
Outputs:
- gradient: float32 [128, 131072], P('vert', 'horiz')
- weighted: float32 [16384], P(('horiz', 'vert'))
The draws below stay inside these ranges and needn't reach their ends.
Inputs may be any that keep to these rules, and one draw needn't show every extreme that they name: block_cols[t, l, b] is a cell tile of the same horiz index as tile t: block_cols[t, l, b] // 128 == t // 16. obs_target is a permutation; an entry held at vert index v targets a position p with (p // 512) % 4 == v; of the 512 entries of one device at most 256 target one horiz index (p // (4 * 512)), and every device sends exactly 256 to one horiz index.
All inputs are finite; a program needn't handle non-finite values.
Results may differ from the reference program's by a relative error of at most 0.0026.
Values may be sent and summed in bfloat16 or wider, within the bound.
No kernel may reach another device: no remote copies, remote signals or barrier semaphores. Data moves between devices by JAX's collectives and lax.ppermute only.
A program may use at most 128 MiB of HBM per device.

```python
import math
import jax
import jax.numpy as jnp
from jax import lax

LEV = 128
TILE = 128
NBL = 2
OT_DEV = 16
CT_DEV = 128
NCELL = 131072
NCT = 1024
OTILES = 128
NOBS = 16384
SLOT_OBS = 512
CAP = 256
N_HORIZ = 8
N_VERT = 4


def draw_block_cols(key, part):
    owner = jnp.arange(OTILES, dtype=jnp.int32) // OT_DEV
    offsets = jax.random.randint(key, (OTILES, LEV, NBL), 0, CT_DEV, dtype=jnp.int32)
    return (owner[:, None, None] * CT_DEV + offsets).astype(jnp.int32)


def draw_obs_target(key, part):
    horiz_count = N_HORIZ
    vert_count = N_VERT
    slot_rows = SLOT_OBS
    capacity = CAP
    base_count = (slot_rows - capacity) // (horiz_count - 1)
    remainder = (slot_rows - capacity) % (horiz_count - 1)
    distance = jnp.arange(horiz_count, dtype=jnp.int32)
    counts = jnp.where(distance == 0, capacity, base_count + (distance - 1 < remainder).astype(jnp.int32)).astype(jnp.int32)
    key_shift, key_place, key_order = jax.random.split(key, 3)
    shifts = jax.random.randint(key_shift, (vert_count,), 0, horiz_count, dtype=jnp.int32)
    ends = jnp.cumsum(counts)
    begins = ends - counts
    entry = jnp.arange(slot_rows, dtype=jnp.int32)
    group = jnp.sum((entry[:, None] >= ends[None, :]).astype(jnp.int32), axis=1)
    within = entry - begins[group]
    source = jnp.arange(horiz_count, dtype=jnp.int32)
    vert_index = jnp.arange(vert_count, dtype=jnp.int32)
    target_dev = (source[None, :, None] + group[None, None, :] + shifts[:, None, None]) % horiz_count
    count_matrix = counts[(source[None, :, None] - source[None, None, :] - shifts[:, None, None]) % horiz_count]
    start_matrix = jnp.cumsum(count_matrix, axis=2) - count_matrix
    first_slot = start_matrix[vert_index[:, None, None], target_dev, source[None, :, None]]
    place_keys = jax.random.split(key_place, vert_count * horiz_count)
    placements = jax.vmap(lambda single: jax.random.permutation(single, slot_rows))(place_keys)
    placements = placements.reshape(vert_count, horiz_count, slot_rows).astype(jnp.int32)
    position = placements[vert_index[:, None, None], target_dev, first_slot + within[None, None, :]]
    target = target_dev * (vert_count * slot_rows) + vert_index[:, None, None] * slot_rows + position
    order_keys = jax.random.split(key_order, vert_count * horiz_count)
    orders = jax.vmap(lambda single: jax.random.permutation(single, slot_rows))(order_keys)
    orders = orders.reshape(vert_count, horiz_count, slot_rows).astype(jnp.int32)
    target = jnp.take_along_axis(target, orders, axis=2)
    return jnp.transpose(target, (1, 0, 2)).reshape(-1).astype(jnp.int32)


def block_levels(key, shape, cuts, low, top_value):
    factor_of = 1.0
    for dim, shards_of in cuts:
        draws = jax.random.uniform(jax.random.fold_in(jax.random.fold_in(key, 6), dim), (shards_of,), jnp.float32, low / len(cuts), top_value / len(cuts))
        factor_of = factor_of * jnp.repeat(jnp.exp(draws), shape[dim] // shards_of).reshape((-1,) + (1,) * (len(shape) - 1 - dim))
    return factor_of


def noise(own_key, extent, width, reach, cuts=(), kind=jnp.bfloat16):
    result = width * jax.random.normal(own_key, extent, jnp.float32)
    if cuts:
        result = result * block_levels(own_key, extent, cuts, -0.22, 0.18)
    return jnp.clip(result, -reach, reach).astype(kind)


def setup_inputs(seed: int = 0) -> dict:
    arg_keys = jax.random.split(jax.random.key(seed), 9)
    chi = noise(arg_keys[0], (LEV, NCELL), 1.0, 6.0, ((0, 4), (1, 8)), jnp.float32)
    bg_std = jnp.clip(jnp.exp(math.log(3.0) - 2.3025851 * jax.random.uniform(arg_keys[1], (LEV, NCELL), jnp.float32) ** block_levels(arg_keys[1], (LEV, NCELL), ((0, 4), (1, 8)), -0.2, 0.2)), 0.3, 3.0)
    vert_root = noise(arg_keys[2], (LEV, LEV), LEV ** -0.5, 0.5, (), jnp.float32)
    obs_blocks = noise(arg_keys[3], (OTILES, LEV, NBL, TILE, TILE), (LEV * NBL * TILE) ** -0.5, 0.03125, ((0, 8), (1, 4)))
    block_cols = draw_block_cols(jax.random.fold_in(arg_keys[8], 71), 0)
    departures = noise(arg_keys[5], (NOBS,), 1.0, 6.0, ((0, 32),), jnp.float32)
    obs_std = jnp.clip(jnp.exp(math.log(2.0) - 1.3862944 * jax.random.uniform(arg_keys[6], (NOBS,), jnp.float32) ** block_levels(arg_keys[6], (NOBS,), ((0, 32),), -0.2, 0.2)), 0.5, 2.0)
    obs_target = draw_obs_target(jax.random.fold_in(arg_keys[8], 71), 0)
    return {"chi": chi, "bg_std": bg_std, "vert_root": vert_root, "obs_blocks": obs_blocks, "block_cols": block_cols, "departures": departures, "obs_std": obs_std, "obs_target": obs_target}


def reference(chi, bg_std, vert_root, obs_blocks, block_cols, departures, obs_std, obs_target):
    highest = lax.Precision.HIGHEST
    mixed_levels = jnp.dot(vert_root, chi, precision=highest, preferred_element_type=jnp.float32)
    increment = (bg_std * mixed_levels).astype(jnp.bfloat16)
    state_tiles = increment.reshape(LEV, NCT, TILE)
    level_index = jnp.arange(LEV)[None, :, None]
    picked = state_tiles[level_index, block_cols]
    blocks_group = obs_blocks.reshape(N_HORIZ, OT_DEV, LEV, NBL, TILE, TILE)
    picked_group = picked.reshape(N_HORIZ, OT_DEV, LEV, NBL, TILE)

    def forward(pair):
        blocks, values = pair
        return jnp.einsum("tlbij,tlbj->ti", blocks.astype(jnp.float32), values.astype(jnp.float32))

    equivalent = lax.map(forward, (blocks_group, picked_group)).reshape(NOBS)
    arranged = jnp.zeros((NOBS,), jnp.float32).at[obs_target].set(departures)
    spread = jnp.zeros((NOBS,), jnp.float32).at[obs_target].set(obs_std)
    weighted = (equivalent - arranged) / (spread * spread)
    wround = weighted.astype(jnp.bfloat16).reshape(N_HORIZ, OT_DEV, TILE)

    def backward(pair):
        blocks, values = pair
        return jnp.einsum("tlbij,ti->tlbj", blocks.astype(jnp.float32), values.astype(jnp.float32))

    contributions = lax.map(backward, (blocks_group, wround)).reshape(OTILES, LEV, NBL, TILE)
    adjoint = jnp.zeros((LEV, NCT, TILE), jnp.float32).at[level_index, block_cols].add(contributions)
    adjoint = adjoint.reshape(LEV, NCELL)
    gradient = chi + jnp.dot(vert_root.T, bg_std * adjoint, precision=highest, preferred_element_type=jnp.float32)
    return gradient, weighted
```

```python
import functools

import jax
import jax.numpy as jnp
from jax import lax
from jax.experimental import pallas as pl
from jax.experimental.pallas import tpu as pltpu
from jax.sharding import PartitionSpec as P

F32 = jnp.float32
BF16 = jnp.bfloat16
GROUP = 16
VMEM = pl.BlockSpec(memory_space=pltpu.VMEM)
SMEM = pl.BlockSpec(memory_space=pltpu.SMEM)


def call(body, outs, inputs, scratch=(), mib=24, flops=0, touched=0):
    return pl.pallas_call(
        body,
        out_shape=outs,
        in_specs=[SMEM] + [VMEM] * (len(inputs) - 1),
        out_specs=[VMEM] * len(outs),
        scratch_shapes=list(scratch),
        compiler_params=pltpu.CompilerParams(vmem_limit_bytes=mib << 20),
        cost_estimate=pl.CostEstimate(flops=flops, bytes_accessed=touched, transcendentals=0),
    )(*inputs)


def high_part(x):
    return x.astype(BF16).astype(F32)


def nt_dot(a, b):
    return lax.dot_general(a, b, (((1,), (1,)), ((), ())), preferred_element_type=F32)


def spread_rows(x):
    row = lax.broadcasted_iota(jnp.int32, x.shape, 0)
    return jnp.concatenate([jnp.where(row == r, x, 0.0).astype(BF16) for r in range(GROUP)], axis=1)


def tree_sum(values):
    while len(values) > 1:
        values = [values[i] + values[i + 1] for i in range(0, len(values), 2)]
    return values[0]


def mix_kernel(levels, pitch, pos, root, chi, high, low, mixed):
    every = root.shape[0]
    width = high.shape[1]
    tiles = chi.shape[1] // width
    lane = lax.broadcasted_iota(jnp.int32, root.shape, 1)
    table = root[...]
    left = jnp.zeros(root.shape, F32)
    for g in range(4):
        own = pltpu.roll(table, (g * levels - pos[0] * levels + every) % every, 1)
        own_high = high_part(own)
        part = own_high if g < 2 else own - own_high
        left = jnp.where(lane // levels == g, part, left)
    left = left[:, : 4 * levels].astype(BF16)
    step = 4

    @pl.loop(0, tiles // step)
    def _(i):
        for u in range(step):
            c = i * step + u
            x = chi[:, pl.ds(pl.multiple_of(c * width, width), width)]
            x_high = high_part(x)
            x_low = x - x_high
            right = jnp.concatenate([x_high, x_low, x_high, x_low], axis=0).astype(BF16)
            mixed[pl.ds(c, every, stride=pitch), :] = jnp.dot(left, right, preferred_element_type=F32)

    @pl.loop(0, every // step)
    def _(i):
        for u in range(step):
            l = i * step + u
            rows = mixed[pl.ds(pl.multiple_of(l * pitch, 8), tiles), :]
            high[pl.ds(pl.multiple_of(l * tiles, tiles), tiles), :] = rows.astype(BF16)

    @pl.loop(0, levels)
    def _(i):
        rows = mixed[pl.ds(pl.multiple_of((pos[0] * levels + i) * pitch, 8), tiles), :]
        low[pl.ds(pl.multiple_of(i * tiles, tiles), tiles), :] = (rows - high_part(rows)).astype(BF16)


def pick_kernel(count, pos, *refs):
    cols = refs[:count]
    high, low, own = refs[count : count + 3]
    outs = refs[count + 3 :]
    levels = cols[0].shape[1]
    tiles = low.shape[0] // levels
    tile = lax.broadcasted_iota(jnp.int32, (cols[0].shape[0], tiles), 1)
    for k in range(count):
        wanted = cols[k][...]
        base = (pos[0] ^ k) * levels * tiles
        for i in range(levels):
            hot = jnp.where(wanted[:, i : i + 1] == tile, 1.0, 0.0).astype(BF16)
            rows = high[pl.ds(pl.multiple_of(base + i * tiles, tiles), tiles), :]
            picked = jnp.dot(hot, rows, preferred_element_type=F32)
            if k == 0:
                own[i] = picked + jnp.dot(hot, low[i * tiles : (i + 1) * tiles, :], preferred_element_type=F32)
            else:
                outs[k - 1][i] = picked.astype(BF16)


def scale_kernel(pitch, pos, cols, bg, out, spaced):
    levels, width = bg.shape[0], out.shape[2]
    tiles = bg.shape[1] // width
    step = 4

    @pl.loop(0, tiles // step)
    def _(i):
        for u in range(step):
            c = i * step + u
            spaced[pl.ds(c, levels, stride=pitch), :] = bg[:, pl.ds(pl.multiple_of(c * width, width), width)]

    tile = lax.broadcasted_iota(jnp.int32, (cols.shape[0], tiles), 1)
    wanted = cols[...]
    for i in range(levels):
        hot = jnp.where(wanted[:, i : i + 1] == tile, 1.0, 0.0).astype(BF16)
        rows = spaced[i * pitch : i * pitch + tiles, :]
        first = high_part(rows)
        second = high_part(rows - first)
        third = rows - first - second
        parts = jnp.concatenate([first, second, third], axis=1).astype(BF16)
        picked = jnp.dot(hot, parts, preferred_element_type=F32)
        out[i] = picked[:, :width] + picked[:, width : 2 * width] + picked[:, 2 * width :]


def place_kernel(count, rows, pos, *refs):
    entries, out = refs[:count], refs[count]
    width = out.shape[2]
    index = lax.broadcasted_iota(jnp.int32, (6 * rows, width), 0)
    term, slot = index // rows, index % rows
    place = lax.broadcasted_iota(jnp.int32, (width, width), 0)
    total = jnp.zeros((6 * rows, width), F32)
    for entry in entries:
        for e in range(entry.shape[1]):
            target = entry[2, e : e + 1, :].astype(jnp.int32) - pos[1]
            left = jnp.zeros((6 * rows, width), F32)
            for which in range(2):
                value = entry[which, e : e + 1, :]
                first = high_part(value)
                second = high_part(value - first)
                for n, part in enumerate((first, second, value - first - second)):
                    left = jnp.where(term == 3 * which + n, part, left)
            left = jnp.where(slot == target // width, left, 0.0).astype(BF16)
            hot = jnp.where(target % width == place, 1.0, 0.0).astype(BF16)
            total += nt_dot(left, hot)
    for which in range(2):
        base = 3 * which * rows
        out[which] = total[base : base + rows] + total[base + rows : base + 2 * rows] + total[base + 2 * rows : base + 3 * rows]


def forward_kernel(count, pos, *refs):
    placed, scale, own = refs[:3]
    others = refs[3 : 2 + count]
    blocks, out, spare = refs[2 + count :]
    tiles, levels, per, width, _ = blocks.shape
    picks = tiles * per

    def level(l, totals):
        mixed = own[l]
        for other in others:
            mixed = mixed + other[l].astype(F32)
        values = high_part(scale[l] * mixed)
        result = []
        for h in range(picks // GROUP):
            left = spread_rows(values[h * GROUP : (h + 1) * GROUP])
            right = jnp.concatenate(
                [blocks[(h * GROUP + r) // per, l, (h * GROUP + r) % per] for r in range(GROUP)], axis=1
            )
            result.append(totals[h] + nt_dot(left, right))
        return tuple(result)

    zero = jnp.zeros((GROUP, width), F32)
    totals = lax.fori_loop(0, levels, level, (zero,) * (picks // GROUP))
    for h, total in enumerate(totals):
        spare[h * GROUP : (h + 1) * GROUP, :] = total
    equivalent = spare[pl.ds(0, tiles, stride=per), :]
    for b in range(1, per):
        equivalent = equivalent + spare[pl.ds(b, tiles, stride=per), :]
    out[0] = equivalent - placed[0]
    out[1] = placed[1]


def backward_kernel(count, pos, *refs):
    partials = refs[:count]
    scale, blocks, weighted, out, spare = refs[count:]
    tiles, levels, per, width, _ = blocks.shape
    picks = tiles * per
    excess = tree_sum([partial[0] for partial in partials])
    error = tree_sum([partial[1] for partial in partials])
    weights = excess / (error * error)
    weighted[...] = weights
    rounded = high_part(weights)
    for b in range(per):
        spare[pl.ds(b, tiles, stride=per), :] = rounded
    lefts = [spread_rows(spare[h * GROUP : (h + 1) * GROUP, :]) for h in range(picks // GROUP)]

    @pl.loop(0, levels)
    def _(l):
        for h, left in enumerate(lefts):
            right = jnp.concatenate(
                [blocks[(h * GROUP + r) // per, l, (h * GROUP + r) % per] for r in range(GROUP)], axis=0
            )
            sent = jnp.dot(left, right, preferred_element_type=F32)
            part = pl.ds(h * GROUP, GROUP)
            out[l, part, :] = (scale[l, part, :] * sent).astype(BF16)


def gradient_kernel(count, pitch, pos, *refs):
    root, chi = refs[:2]
    cols, sent = refs[2 : 2 + count], refs[2 + count : 2 + 2 * count]
    out, adjoint, turned = refs[2 + 2 * count :]
    levels, width = chi.shape[0], sent[0].shape[2]
    tiles = chi.shape[1] // width
    every = root.shape[0]
    tile = lax.broadcasted_iota(jnp.int32, (tiles, cols[0].shape[1]), 0)
    turned[...] = root[...].T
    for k in range(count):
        base = (pos[0] ^ k) * levels * pitch

        @pl.loop(0, levels // 8)
        def _(g):
            wanted = cols[k][pl.ds(pl.multiple_of(g * 8, 8), 8), :]
            for u in range(8):
                i = g * 8 + u
                hot = jnp.where(wanted[u : u + 1, :] == tile, 1.0, 0.0).astype(BF16)
                total = jnp.dot(hot, sent[k][i], preferred_element_type=F32)
                adjoint[pl.ds(pl.multiple_of(base + i * pitch, 8), tiles), :] = total

    own = turned[pl.ds(pl.multiple_of(pos[0] * levels, 8), levels), :]
    own_high = high_part(own)
    own_low = own - own_high
    left = jnp.concatenate(
        [jnp.concatenate([own_high, own_high], axis=1), jnp.concatenate([own_low, own_low], axis=1)], axis=0
    ).astype(BF16)
    step = 4

    @pl.loop(0, tiles // step)
    def _(i):
        for u in range(step):
            c = i * step + u
            rows = adjoint[pl.ds(c, every, stride=pitch), :]
            first = high_part(rows)
            right = jnp.concatenate([first, rows - first], axis=0).astype(BF16)
            both = jnp.dot(left, right, preferred_element_type=F32)
            part = pl.ds(pl.multiple_of(c * width, width), width)
            out[:, part] = chi[:, part] + (both[:levels] + both[levels:])


def exchange(x, axis, size, k):
    return lax.ppermute(x, axis, [(i, i ^ k) for i in range(size)])


def local(chi, bg_std, vert_root, obs_blocks, block_cols, departures, obs_std, obs_target):
    own_tiles, levels, per, width, _ = obs_blocks.shape
    cell_count = chi.shape[1]
    tiles = cell_count // width
    every = vert_root.shape[0]
    slot_rows = departures.shape[0]
    picks = own_tiles * per
    horiz = lax.axis_size("horiz")
    vert = lax.axis_size("vert")
    vert_pos = lax.axis_index("vert").astype(jnp.int32)
    horiz_pos = lax.axis_index("horiz").astype(jnp.int32)
    pitch = tiles + 8
    pos = jnp.stack([vert_pos, horiz_pos * (vert * slot_rows)])

    cols = jnp.transpose(block_cols - horiz_pos * tiles, (0, 2, 1)).reshape(picks, levels)
    all_cols = [cols] + [exchange(cols, "vert", vert, k) for k in range(1, vert)]

    high, low = call(
        functools.partial(mix_kernel, levels, pitch),
        (jax.ShapeDtypeStruct((every * tiles, width), BF16), jax.ShapeDtypeStruct((levels * tiles, width), BF16)),
        (pos, vert_root, chi),
        [pltpu.VMEM((every * pitch, width), F32)],
        flops=8 * every * levels * cell_count,
        touched=4 * every * cell_count,
    )
    picked_shape = (levels, picks, width)
    own_picks, *sent_picks = call(
        functools.partial(pick_kernel, vert),
        (jax.ShapeDtypeStruct(picked_shape, F32),) + (jax.ShapeDtypeStruct(picked_shape, BF16),) * (vert - 1),
        (pos, *all_cols, high, low),
        flops=2 * every * picks * tiles * width,
        touched=4 * every * cell_count,
    )
    got_picks = [exchange(x, "vert", vert, k + 1) for k, x in enumerate(sent_picks)]

    entry_rows = slot_rows // width
    entries = jnp.stack([departures, obs_std, obs_target.astype(F32)]).reshape(3, entry_rows, width)
    all_entries = [entries] + [exchange(entries, "horiz", horiz, k) for k in range(1, horiz)]
    (scale,) = call(
        functools.partial(scale_kernel, pitch),
        (jax.ShapeDtypeStruct(picked_shape, F32),),
        (pos, cols, bg_std),
        [pltpu.VMEM((levels * pitch, width), F32)],
        flops=6 * levels * picks * tiles * width,
        touched=8 * levels * cell_count,
    )
    (placed,) = call(
        functools.partial(place_kernel, horiz, own_tiles),
        (jax.ShapeDtypeStruct((2, own_tiles, width), F32),),
        (pos, *all_entries),
        touched=1 << 20,
    )
    blocks = pltpu.with_memory_space_constraint(obs_blocks, pltpu.VMEM)
    block_bytes = 2 * obs_blocks.size
    (partial,) = call(
        functools.partial(forward_kernel, vert),
        (jax.ShapeDtypeStruct((2, own_tiles, width), F32),),
        (pos, placed, scale, own_picks, *got_picks, blocks),
        [pltpu.VMEM((picks, width), F32)],
        flops=2 * obs_blocks.size,
        touched=block_bytes,
    )
    partials = [partial] + [exchange(partial, "vert", vert, k) for k in range(1, vert)]
    all_weights, sent = call(
        functools.partial(backward_kernel, vert),
        (jax.ShapeDtypeStruct((own_tiles, width), F32), jax.ShapeDtypeStruct(picked_shape, BF16)),
        (pos, *partials, scale, blocks),
        [pltpu.VMEM((picks, width), F32)],
        flops=2 * obs_blocks.size,
        touched=block_bytes,
    )
    all_sent = [sent] + [exchange(sent, "vert", vert, k) for k in range(1, vert)]
    weighted = lax.dynamic_slice_in_dim(all_weights.reshape(own_tiles * width), vert_pos * slot_rows, slot_rows, 0)
    (gradient,) = call(
        functools.partial(gradient_kernel, vert, pitch),
        (jax.ShapeDtypeStruct(chi.shape, F32),),
        (pos, vert_root, chi, *[x.T for x in all_cols], *all_sent),
        [pltpu.VMEM((every * pitch, width), F32), pltpu.VMEM((every, every), F32)],
        flops=8 * every * levels * cell_count,
        touched=4 * every * cell_count,
    )
    return gradient, weighted


def solution(mesh):
    in_specs = (
        P("vert", "horiz"),
        P("vert", "horiz"),
        P(),
        P("horiz", "vert", None, None, None),
        P("horiz", "vert", None),
        P(("horiz", "vert")),
        P(("horiz", "vert")),
        P(("horiz", "vert")),
    )
    out_specs = (P("vert", "horiz"), P(("horiz", "vert")))
    return jax.shard_map(local, mesh=mesh, in_specs=in_specs, out_specs=out_specs, check_vma=False)
```

```python
import functools

import jax
import jax.numpy as jnp
from jax import lax
from jax.experimental import pallas as pl
from jax.experimental.pallas import tpu as pltpu
from jax.sharding import PartitionSpec as P

F32 = jnp.float32
BF16 = jnp.bfloat16
GROUP = 16
MIX_STEP = 32
SCALE_STEP = 32
GRAD_STEP = 32
HOT_STEP = 32
LEVEL_STEP = 8
PIECES = 8
PARTS = 4
VMEM = pl.BlockSpec(memory_space=pltpu.VMEM)
SMEM = pl.BlockSpec(memory_space=pltpu.SMEM)
HBM = pl.BlockSpec(memory_space=pl.ANY)


def call(body, outs, inputs, scratch=(), mib=2, flops=0, touched=0, left=(), pinned=True):
    inputs = [
        x if i == 0 else pltpu.with_memory_space_constraint(x, pltpu.HBM if i in left else pltpu.VMEM)
        for i, x in enumerate(inputs)
    ]
    outs = [pltpu.VMEM(x.shape, x.dtype) if pinned else x for x in outs]
    return pl.pallas_call(
        body,
        out_shape=outs,
        in_specs=[SMEM] + [HBM if i in left else VMEM for i in range(1, len(inputs))],
        out_specs=[VMEM] * len(outs),
        scratch_shapes=list(scratch),
        compiler_params=pltpu.CompilerParams(vmem_limit_bytes=mib << 20),
        cost_estimate=pl.CostEstimate(flops=flops, bytes_accessed=touched, transcendentals=0),
    )(*inputs)


def high_part(x):
    return x.astype(BF16).astype(F32)


def nt_dot(a, b):
    return lax.dot_general(a, b, (((1,), (1,)), ((), ())), preferred_element_type=F32)


def spread_rows(x):
    row = lax.broadcasted_iota(jnp.int32, x.shape, 0)
    return jnp.concatenate([jnp.where(row == r, x, 0.0).astype(BF16) for r in range(GROUP)], axis=1)


def tree_sum(values):
    while len(values) > 1:
        values = [values[i] + values[i + 1] for i in range(0, len(values), 2)]
    return values[0]


def mix_kernel(levels, pitch, pos, root, chi_hbm, high, low, mixed, chi, arrived):
    every = root.shape[0]
    width = high.shape[1]
    tiles = chi.shape[1] // width
    step = MIX_STEP
    pieces = tiles // step

    def fetch(i):
        part = pl.ds(pl.multiple_of(i * step * width, step * width), step * width)
        return pltpu.make_async_copy(chi_hbm.at[:, part], chi.at[:, part], arrived.at[i])

    for i in range(pieces):
        fetch(i).start()
    lane = lax.broadcasted_iota(jnp.int32, root.shape, 1)
    table = root[...]
    left = jnp.zeros(root.shape, F32)
    for g in range(4):
        own = pltpu.roll(table, (g * levels - pos[0] * levels + every) % every, 1)
        own_high = high_part(own)
        part = own_high if g < 2 else own - own_high
        left = jnp.where(lane // levels == g, part, left)
    left = left[:, : 4 * levels].astype(BF16)

    @pl.loop(0, pieces)
    def _(i):
        fetch(i).wait()
        for u in range(step):
            c = i * step + u
            x = chi[:, pl.ds(pl.multiple_of(c * width, width), width)]
            x_high = high_part(x)
            x_low = x - x_high
            right = jnp.concatenate([x_high, x_low, x_high, x_low], axis=0).astype(BF16)
            mixed[pl.ds(c, every, stride=pitch), :] = jnp.dot(left, right, preferred_element_type=F32)

    @pl.loop(0, every // step)
    def _(i):
        for u in range(step):
            l = i * step + u
            rows = mixed[pl.ds(pl.multiple_of(l * pitch, 8), tiles), :]
            high[pl.ds(pl.multiple_of(l * tiles, tiles), tiles), :] = rows.astype(BF16)

    @pl.loop(0, levels)
    def _(i):
        rows = mixed[pl.ds(pl.multiple_of((pos[0] * levels + i) * pitch, 8), tiles), :]
        low[pl.ds(pl.multiple_of(i * tiles, tiles), tiles), :] = (rows - high_part(rows)).astype(BF16)


def pick_kernel(count, pos, *refs):
    cols = refs[:count]
    high, low, own = refs[count : count + 3]
    outs = refs[count + 3 :]
    levels = cols[0].shape[1]
    tiles = low.shape[0] // levels
    tile = lax.broadcasted_iota(jnp.int32, (cols[0].shape[0], tiles), 1)
    for k in range(count):
        wanted = cols[k][...]
        base = (pos[0] ^ k) * levels * tiles
        for i in range(levels):
            hot = jnp.where(wanted[:, i : i + 1] == tile, 1.0, 0.0).astype(BF16)
            rows = high[pl.ds(pl.multiple_of(base + i * tiles, tiles), tiles), :]
            picked = jnp.dot(hot, rows, preferred_element_type=F32)
            if k == 0:
                own[i] = picked + jnp.dot(hot, low[i * tiles : (i + 1) * tiles, :], preferred_element_type=F32)
            else:
                outs[k - 1][i] = picked.astype(BF16)


def load_kernel(pitch, pos, cols, bg_hbm, blocks_hbm, *refs):
    parts = refs[:PARTS]
    out, spaced, bg, arrived = refs[PARTS:]
    span = blocks_hbm.shape[0] // PIECES
    each = PIECES // PARTS
    bg_copy = pltpu.make_async_copy(bg_hbm, bg, arrived.at[PIECES])
    bg_copy.start()
    copies = []
    for n in range(PIECES):
        part = pl.ds(n * span, span)
        there = parts[n // each].at[pl.ds(n % each * span, span)]
        copies.append(pltpu.make_async_copy(blocks_hbm.at[part], there, arrived.at[n]))
        copies[n].start()
    levels, width = bg.shape[0], out.shape[2]
    tiles = bg.shape[1] // width
    step = SCALE_STEP
    bg_copy.wait()

    @pl.loop(0, tiles // step)
    def _(i):
        for u in range(step):
            c = i * step + u
            spaced[pl.ds(c, levels, stride=pitch), :] = bg[:, pl.ds(pl.multiple_of(c * width, width), width)]

    tile = lax.broadcasted_iota(jnp.int32, (cols.shape[0], tiles), 1)
    wanted = cols[...]
    for i in range(levels):
        hot = jnp.where(wanted[:, i : i + 1] == tile, 1.0, 0.0).astype(BF16)
        rows = spaced[i * pitch : i * pitch + tiles, :]
        first = high_part(rows)
        second = high_part(rows - first)
        third = rows - first - second
        parts = jnp.concatenate([first, second, third], axis=1).astype(BF16)
        picked = jnp.dot(hot, parts, preferred_element_type=F32)
        out[i] = picked[:, :width] + picked[:, width : 2 * width] + picked[:, 2 * width :]
    for copy in copies:
        copy.wait()


def place_kernel(rows, pos, entries, out):
    width = out.shape[2]
    index = lax.broadcasted_iota(jnp.int32, (6 * rows, width), 0)
    term, slot = index // rows, index % rows
    place = lax.broadcasted_iota(jnp.int32, (width, width), 0)
    total = jnp.zeros((6 * rows, width), F32)
    for n in range(entries.shape[0]):
        entry = entries.at[n]
        for e in range(entry.shape[1]):
            target = entry[2, e : e + 1, :].astype(jnp.int32) - pos[1]
            left = jnp.zeros((6 * rows, width), F32)
            for which in range(2):
                value = entry[which, e : e + 1, :]
                first = high_part(value)
                second = high_part(value - first)
                for m, part in enumerate((first, second, value - first - second)):
                    left = jnp.where(term == 3 * which + m, part, left)
            left = jnp.where(slot == target // width, left, 0.0).astype(BF16)
            hot = jnp.where(target % width == place, 1.0, 0.0).astype(BF16)
            total += nt_dot(left, hot)
    for which in range(2):
        base = 3 * which * rows
        out[which] = total[base : base + rows] + total[base + rows : base + 2 * rows] + total[base + 2 * rows : base + 3 * rows]


def block_sizes(blocks):
    tiles, levels, per, width, _ = blocks[0].shape
    return tiles * len(blocks), levels, per, width


def block(blocks, t, l, b):
    tiles = blocks[0].shape[0]
    return blocks[t // tiles][t % tiles, l, b]


def forward_kernel(count, pos, *refs):
    placed, scale, own = refs[:3]
    others = refs[3 : 2 + count]
    *blocks, out, spare = refs[2 + count :]
    tiles, levels, per, width = block_sizes(blocks)
    picks = tiles * per

    def level(i, totals):
        for u in range(LEVEL_STEP):
            totals = one_level(i * LEVEL_STEP + u, totals)
        return totals

    def one_level(l, totals):
        mixed = own[l]
        for other in others:
            mixed = mixed + other[l].astype(F32)
        values = high_part(scale[l] * mixed)
        result = []
        for h in range(picks // GROUP):
            left = spread_rows(values[h * GROUP : (h + 1) * GROUP])
            right = jnp.concatenate(
                [block(blocks, (h * GROUP + r) // per, l, (h * GROUP + r) % per) for r in range(GROUP)], axis=1
            )
            result.append(totals[h] + nt_dot(left, right))
        return tuple(result)

    zero = jnp.zeros((GROUP, width), F32)
    totals = lax.fori_loop(0, levels // LEVEL_STEP, level, (zero,) * (picks // GROUP))
    for h, total in enumerate(totals):
        spare[h * GROUP : (h + 1) * GROUP, :] = total
    equivalent = spare[pl.ds(0, tiles, stride=per), :]
    for b in range(1, per):
        equivalent = equivalent + spare[pl.ds(b, tiles, stride=per), :]
    out[0] = equivalent - placed[0]
    out[1] = placed[1]


def backward_kernel(count, pos, *refs):
    partials = refs[:count]
    scale, *blocks, weighted, out, spare, parts = refs[count:]
    tiles, levels, per, width = block_sizes(blocks)
    picks = tiles * per
    excess = tree_sum([partial[0] for partial in partials])
    error = tree_sum([partial[1] for partial in partials])
    weights = excess / (error * error)
    rows = weighted.shape[0]
    for v in range(count):
        parts[v] = weights[v * rows : (v + 1) * rows]
    weighted[...] = parts[pos[0]]
    rounded = high_part(weights)
    for b in range(per):
        spare[pl.ds(b, tiles, stride=per), :] = rounded
    lefts = [spread_rows(spare[h * GROUP : (h + 1) * GROUP, :]) for h in range(picks // GROUP)]

    @pl.loop(0, levels // LEVEL_STEP)
    def _(i):
        for u in range(LEVEL_STEP):
            l = i * LEVEL_STEP + u
            for h, left in enumerate(lefts):
                right = jnp.concatenate(
                    [block(blocks, (h * GROUP + r) // per, l, (h * GROUP + r) % per) for r in range(GROUP)], axis=0
                )
                sent = jnp.dot(left, right, preferred_element_type=F32)
                part = pl.ds(h * GROUP, GROUP)
                out[l, part, :] = (scale[l, part, :] * sent).astype(BF16)


def gradient_kernel(count, pitch, pos, *refs):
    root, chi = refs[:2]
    cols, sent = refs[2 : 2 + count], refs[2 + count : 2 + 2 * count]
    out, adjoint, turned, flipped = refs[2 + 2 * count :]
    levels, width = chi.shape[0], sent[0].shape[2]
    tiles = chi.shape[1] // width
    every = root.shape[0]
    tile = lax.broadcasted_iota(jnp.int32, (tiles, cols[0].shape[0]), 0)
    turned[...] = root[...].T
    hot_step = min(HOT_STEP, levels)
    for k in range(count):
        base = (pos[0] ^ k) * levels * pitch
        flipped[...] = cols[k][...].T

        @pl.loop(0, levels // hot_step)
        def _(g):
            wanted = flipped[pl.ds(pl.multiple_of(g * hot_step, hot_step), hot_step), :]
            for u in range(hot_step):
                i = g * hot_step + u
                hot = jnp.where(wanted[u : u + 1, :] == tile, 1.0, 0.0).astype(BF16)
                total = jnp.dot(hot, sent[k][i], preferred_element_type=F32)
                adjoint[pl.ds(pl.multiple_of(base + i * pitch, 8), tiles), :] = total

    own = turned[pl.ds(pl.multiple_of(pos[0] * levels, 8), levels), :]
    own_high = high_part(own)
    own_low = own - own_high
    left = jnp.concatenate(
        [jnp.concatenate([own_high, own_high], axis=1), jnp.concatenate([own_low, own_low], axis=1)], axis=0
    ).astype(BF16)
    step = GRAD_STEP

    @pl.loop(0, tiles // step)
    def _(i):
        for u in range(step):
            c = i * step + u
            rows = adjoint[pl.ds(c, every, stride=pitch), :]
            first = high_part(rows)
            right = jnp.concatenate([first, rows - first], axis=0).astype(BF16)
            both = jnp.dot(left, right, preferred_element_type=F32)
            part = pl.ds(pl.multiple_of(c * width, width), width)
            out[:, part] = chi[:, part] + (both[:levels] + both[levels:])


def exchange(x, axis, size, k):
    return lax.ppermute(x, axis, [(i, i ^ k) for i in range(size)])


def local(chi, bg_std, vert_root, obs_blocks, block_cols, departures, obs_std, obs_target):
    own_tiles, levels, per, width, _ = obs_blocks.shape
    cell_count = chi.shape[1]
    tiles = cell_count // width
    every = vert_root.shape[0]
    slot_rows = departures.shape[0]
    picks = own_tiles * per
    horiz = lax.axis_size("horiz")
    vert = lax.axis_size("vert")
    vert_pos = lax.axis_index("vert").astype(jnp.int32)
    horiz_pos = lax.axis_index("horiz").astype(jnp.int32)
    pitch = tiles + 8
    pos = jnp.stack([vert_pos, horiz_pos * (vert * slot_rows)])

    cols = jnp.transpose(block_cols - horiz_pos * tiles, (0, 2, 1)).reshape(picks, levels)
    all_cols = [cols] + [exchange(cols, "vert", vert, k) for k in range(1, vert)]

    high, low = call(
        functools.partial(mix_kernel, levels, pitch),
        (jax.ShapeDtypeStruct((every * tiles, width), BF16), jax.ShapeDtypeStruct((levels * tiles, width), BF16)),
        (pos, vert_root, chi),
        [
            pltpu.VMEM((every * pitch, width), F32),
            pltpu.VMEM(chi.shape, F32),
            pltpu.SemaphoreType.DMA((tiles // MIX_STEP,)),
        ],
        left=(2,),
        mib=12,
        flops=8 * every * levels * cell_count,
        touched=4 * every * cell_count,
    )
    picked_shape = (levels, picks, width)
    own_picks, *sent_picks = call(
        functools.partial(pick_kernel, vert),
        (jax.ShapeDtypeStruct(picked_shape, F32),) + (jax.ShapeDtypeStruct(picked_shape, BF16),) * (vert - 1),
        (pos, *all_cols, high, low),
        flops=2 * every * picks * tiles * width,
        touched=4 * every * cell_count,
    )

    entry_rows = slot_rows // width
    entries = jnp.stack([departures, obs_std, obs_target.astype(F32)]).reshape(1, 3, entry_rows, width)
    hop = 1
    while hop < horiz:
        entries = jnp.concatenate([entries, exchange(entries, "horiz", horiz, hop)], axis=0)
        hop *= 2
    obs_blocks, *sent_picks = lax.optimization_barrier((obs_blocks, *sent_picks))
    got_picks = [exchange(x, "vert", vert, k + 1) for k, x in enumerate(sent_picks)]
    *blocks, scale = call(
        functools.partial(load_kernel, pitch),
        (jax.ShapeDtypeStruct((own_tiles // PARTS, *obs_blocks.shape[1:]), BF16),) * PARTS
        + (jax.ShapeDtypeStruct(picked_shape, F32),),
        (pos, cols, bg_std, obs_blocks),
        [
            pltpu.VMEM((levels * pitch, width), F32),
            pltpu.VMEM(bg_std.shape, F32),
            pltpu.SemaphoreType.DMA((PIECES + 1,)),
        ],
        left=(2, 3),
        mib=12,
        flops=6 * levels * picks * tiles * width,
        touched=4 * obs_blocks.size,
    )
    (placed,) = call(
        functools.partial(place_kernel, own_tiles),
        (jax.ShapeDtypeStruct((2, own_tiles, width), F32),),
        (pos, entries),
        touched=1 << 20,
    )
    block_bytes = 2 * obs_blocks.size
    (partial,) = call(
        functools.partial(forward_kernel, vert),
        (jax.ShapeDtypeStruct((2, own_tiles, width), F32),),
        (pos, placed, scale, own_picks, *got_picks, *blocks),
        [pltpu.VMEM((picks, width), F32)],
        flops=2 * obs_blocks.size,
        touched=block_bytes,
    )
    partials = [partial] + [exchange(partial, "vert", vert, k) for k in range(1, vert)]
    weighted, sent = call(
        functools.partial(backward_kernel, vert),
        (jax.ShapeDtypeStruct((entry_rows, width), F32), jax.ShapeDtypeStruct(picked_shape, BF16)),
        (pos, *partials, scale, *blocks),
        [pltpu.VMEM((picks, width), F32), pltpu.VMEM((vert, entry_rows, width), F32)],
        flops=2 * obs_blocks.size,
        touched=block_bytes,
    )
    all_sent = [sent] + [exchange(sent, "vert", vert, k) for k in range(1, vert)]
    (gradient,) = call(
        functools.partial(gradient_kernel, vert, pitch),
        (jax.ShapeDtypeStruct(chi.shape, F32),),
        (pos, vert_root, chi, *all_cols, *all_sent),
        [pltpu.VMEM((every * pitch, width), F32), pltpu.VMEM((every, every), F32), pltpu.VMEM((levels, picks), jnp.int32)],
        mib=14,
        pinned=False,
        flops=8 * every * levels * cell_count,
        touched=4 * every * cell_count,
    )
    return gradient, weighted.reshape(slot_rows)


def solution(mesh):
    in_specs = (
        P("vert", "horiz"),
        P("vert", "horiz"),
        P(),
        P("horiz", "vert", None, None, None),
        P("horiz", "vert", None),
        P(("horiz", "vert")),
        P(("horiz", "vert")),
        P(("horiz", "vert")),
    )
    out_specs = (P("vert", "horiz"), P(("horiz", "vert")))
    return jax.shard_map(local, mesh=mesh, in_specs=in_specs, out_specs=out_specs, check_vma=False)
```

```python
import functools

import jax
import jax.numpy as jnp
from jax import lax
from jax.experimental import pallas as pl
from jax.experimental.pallas import tpu as pltpu
from jax.sharding import PartitionSpec as P

F32 = jnp.float32
BF16 = jnp.bfloat16
GROUP = 16
MIX_STEP = 32
SCALE_STEP = 32
GRAD_STEP = 32
PARTS = 8
SPLIT = 4
IN_MIX = 2
IN_PICK = 1
IN_SCALE = 2
VMEM = pl.BlockSpec(memory_space=pltpu.VMEM)
SMEM = pl.BlockSpec(memory_space=pltpu.SMEM)
HBM = pl.BlockSpec(memory_space=pl.ANY)


def call(body, outs, inputs, scratch=(), mib=2, left=(), outside=(), aliases=None):
    inputs = [
        x if i == 0 else pltpu.with_memory_space_constraint(x, pltpu.HBM if i in left else pltpu.VMEM)
        for i, x in enumerate(inputs)
    ]
    outs = [x if n in outside else pltpu.VMEM(x.shape, x.dtype) for n, x in enumerate(outs)]
    return pl.pallas_call(
        body,
        out_shape=outs,
        in_specs=[SMEM] + [HBM if i in left else VMEM for i in range(1, len(inputs))],
        out_specs=[HBM if n in outside else VMEM for n in range(len(outs))],
        scratch_shapes=list(scratch),
        input_output_aliases=aliases or {},
        compiler_params=pltpu.CompilerParams(vmem_limit_bytes=mib << 20),
        cost_estimate=pl.CostEstimate(flops=1024, bytes_accessed=1024, transcendentals=0),
    )(*inputs)


def high_part(x):
    return x.astype(BF16).astype(F32)


def nt_dot(a, b):
    return lax.dot_general(a, b, (((1,), (1,)), ((), ())), preferred_element_type=F32)


def spread_rows(x):
    row = lax.broadcasted_iota(jnp.int32, x.shape, 0)
    return jnp.concatenate([jnp.where(row == r, x, 0.0).astype(BF16) for r in range(GROUP)], axis=1)


def tree_sum(values):
    while len(values) > 1:
        values = [values[i] + values[i + 1] for i in range(0, len(values), 2)]
    return values[0]


def block_copies(source, parts, first, arrived):
    rows = parts[0].shape[0] // SPLIT
    span = parts[0].shape[1]
    copies = []
    for n, part in enumerate(parts):
        for m in range(SPLIT):
            piece = pl.ds(m * rows, rows)
            there = source.at[piece, pl.ds((first + n) * span, span)]
            copies.append(pltpu.make_async_copy(there, part.at[piece], arrived.at[n * SPLIT + m]))
    return copies


def pack_kernel(pos, table_hbm, value_hbm, error_hbm, target_hbm, cols, entries, table, target, arrived):
    copies = [
        pltpu.make_async_copy(table_hbm, table, arrived.at[0]),
        pltpu.make_async_copy(value_hbm, entries.at[0, 0], arrived.at[1]),
        pltpu.make_async_copy(error_hbm, entries.at[0, 1], arrived.at[2]),
        pltpu.make_async_copy(target_hbm, target, arrived.at[3]),
    ]
    for copy in copies:
        copy.start()
    for copy in copies:
        copy.wait()
    per = table.shape[1]
    for t in range(table.shape[0]):
        cols[t * per : (t + 1) * per, :] = table[t] - pos[2]
    entries[0, 2] = target[...].astype(F32)


def mix_kernel(levels, pitch, pos, root_hbm, chi_hbm, bg_hbm, blocks_hbm, high, low, bg, *refs):
    *parts, mixed, root, chi, arrived, bg_arrived, blocks_arrived = refs
    every = root.shape[0]
    width = high.shape[1]
    tiles = chi.shape[1] // width
    step = MIX_STEP
    pieces = tiles // step

    def fetch(i):
        part = pl.ds(pl.multiple_of(i * step * width, step * width), step * width)
        return pltpu.make_async_copy(chi_hbm.at[:, part], chi.at[:, part], arrived.at[i])

    root_copy = pltpu.make_async_copy(root_hbm, root, arrived.at[pieces])
    root_copy.start()
    for i in range(pieces):
        fetch(i).start()
    copies = [pltpu.make_async_copy(bg_hbm, bg, bg_arrived)] + block_copies(blocks_hbm, parts, 0, blocks_arrived)
    root_copy.wait()
    lane = lax.broadcasted_iota(jnp.int32, root.shape, 1)
    table = root[...]
    left = jnp.zeros(root.shape, F32)
    for g in range(4):
        own = pltpu.roll(table, (g * levels - pos[0] * levels + every) % every, 1)
        own_high = high_part(own)
        part = own_high if g < 2 else own - own_high
        left = jnp.where(lane // levels == g, part, left)
    left = left[:, : 4 * levels].astype(BF16)

    @pl.loop(0, pieces)
    def _(i):
        fetch(i).wait()

        @pl.when(i == 0)
        def _():
            for copy in copies:
                copy.start()

        for u in range(step):
            c = i * step + u
            x = chi[:, pl.ds(pl.multiple_of(c * width, width), width)]
            x_high = high_part(x)
            x_low = x - x_high
            right = jnp.concatenate([x_high, x_low, x_high, x_low], axis=0).astype(BF16)
            mixed[pl.ds(c, every, stride=pitch), :] = jnp.dot(left, right, preferred_element_type=F32)

    @pl.loop(0, every // step)
    def _(i):
        for u in range(step):
            l = i * step + u
            rows = mixed[pl.ds(pl.multiple_of(l * pitch, 8), tiles), :]
            high[pl.ds(pl.multiple_of(l * tiles, tiles), tiles), :] = rows.astype(BF16)

    @pl.loop(0, levels)
    def _(i):
        rows = mixed[pl.ds(pl.multiple_of((pos[0] * levels + i) * pitch, 8), tiles), :]
        low[pl.ds(pl.multiple_of(i * tiles, tiles), tiles), :] = (rows - high_part(rows)).astype(BF16)

    for copy in copies:
        copy.wait()


def pick_kernel(count, pos, *refs):
    cols = refs[:count]
    high, low, entries, received, blocks_hbm, own, joined = refs[count : count + 7]
    *outs, block_arrived = refs[count + 7 :]
    copies = block_copies(blocks_hbm, outs[count - 1 :], IN_MIX, block_arrived)
    for copy in copies:
        copy.start()
    joined[:1] = entries[...]
    joined[1:] = received[...]
    levels = cols[0].shape[1]
    tiles = low.shape[0] // levels
    tile = lax.broadcasted_iota(jnp.int32, (cols[0].shape[0], tiles), 1)

    @pl.when(pos[0] >= 0)
    def _():
        for k in range(count):
            wanted = cols[k][...]
            base = (pos[0] ^ k) * levels * tiles
            for i in range(levels):
                hot = jnp.where(wanted[:, i : i + 1] == tile, 1.0, 0.0).astype(BF16)
                rows = high[pl.ds(pl.multiple_of(base + i * tiles, tiles), tiles), :]
                picked = jnp.dot(hot, rows, preferred_element_type=F32)
                if k == 0:
                    rows = low[i * tiles : (i + 1) * tiles, :]
                    own[i] = picked + jnp.dot(hot, rows, preferred_element_type=F32)
                else:
                    outs[k - 1][i] = picked.astype(BF16)

    for copy in copies:
        copy.wait()


def scale_kernel(pitch, pos, cols, bg, blocks_hbm, out, *refs):
    *parts, spaced, block_arrived = refs
    copies = block_copies(blocks_hbm, parts, IN_MIX + IN_PICK, block_arrived)
    for copy in copies:
        copy.start()
    levels, width = bg.shape[0], out.shape[2]
    tiles = bg.shape[1] // width
    step = SCALE_STEP

    @pl.loop(0, tiles // step)
    def _(i):
        for u in range(step):
            c = i * step + u
            spaced[pl.ds(c, levels, stride=pitch), :] = bg[:, pl.ds(pl.multiple_of(c * width, width), width)]

    tile = lax.broadcasted_iota(jnp.int32, (cols.shape[0], tiles), 1)
    wanted = cols[...]
    for i in range(levels):
        hot = jnp.where(wanted[:, i : i + 1] == tile, 1.0, 0.0).astype(BF16)
        rows = spaced[i * pitch : i * pitch + tiles, :]
        first = high_part(rows)
        second = high_part(rows - first)
        third = rows - first - second
        parts = jnp.concatenate([first, second, third], axis=1).astype(BF16)
        picked = jnp.dot(hot, parts, preferred_element_type=F32)
        out[i] = picked[:, :width] + picked[:, width : 2 * width] + picked[:, 2 * width :]
    for copy in copies:
        copy.wait()


def place_kernel(rows, pos, *refs):
    *groups, out = refs
    width = out.shape[2]
    index = lax.broadcasted_iota(jnp.int32, (6 * rows, width), 0)
    term, slot = index // rows, index % rows
    place = lax.broadcasted_iota(jnp.int32, (width, width), 0)
    total = jnp.zeros((6 * rows, width), F32)
    for entry in [group.at[n] for group in groups for n in range(group.shape[0])]:
        for e in range(entry.shape[1]):
            target = entry[2, e : e + 1, :].astype(jnp.int32) - pos[1]
            left = jnp.zeros((6 * rows, width), F32)
            for which in range(2):
                value = entry[which, e : e + 1, :]
                first = high_part(value)
                second = high_part(value - first)
                for m, part in enumerate((first, second, value - first - second)):
                    left = jnp.where(term == 3 * which + m, part, left)
            left = jnp.where(slot == target // width, left, 0.0).astype(BF16)
            hot = jnp.where(target % width == place, 1.0, 0.0).astype(BF16)
            total += nt_dot(left, hot)
    for which in range(2):
        base = 3 * which * rows
        out[which] = total[base : base + rows] + total[base + rows : base + 2 * rows] + total[base + 2 * rows : base + 3 * rows]


def forward_kernel(count, pos, placed, scale, own, *refs):
    others, refs = refs[: count - 1], refs[count - 1 :]
    held = IN_MIX + IN_PICK + IN_SCALE
    early, (blocks_hbm, out, *late) = refs[:held], refs[held:-2]
    spare, arrived = refs[-2:]
    copies = block_copies(blocks_hbm, late, held, arrived)
    for copy in copies:
        copy.start()
    tiles, span, per, width, _ = early[0].shape
    groups = tiles * per // GROUP
    spare[...] = jnp.zeros_like(spare)
    for n, part in enumerate((*early, *late)):
        for copy in copies[max(n - held, 0) * SPLIT : max(n - held + 1, 0) * SPLIT]:
            copy.wait()

        @pl.when(pos[0] >= 0)
        def _():
            totals = [spare[h * GROUP : (h + 1) * GROUP, :] for h in range(groups)]
            for u in range(span):
                l = n * span + u
                mixed = own[l]
                for other in others:
                    mixed = mixed + other[l].astype(F32)
                values = high_part(scale[l] * mixed)
                for h in range(groups):
                    left = spread_rows(values[h * GROUP : (h + 1) * GROUP])
                    right = jnp.concatenate(
                        [part[(h * GROUP + r) // per, u, r % per] for r in range(GROUP)], axis=1
                    )
                    totals[h] = totals[h] + nt_dot(left, right)
            for h, total in enumerate(totals):
                spare[h * GROUP : (h + 1) * GROUP, :] = total

    total = spare[pl.ds(0, tiles, stride=per), :]
    for b in range(1, per):
        total = total + spare[pl.ds(b, tiles, stride=per), :]
    out[0] = total - placed[0]
    out[1] = placed[1]


def backward_kernel(count, half, pos, *refs):
    partials = refs[:count]
    scale, *blocks, weighted, out, spare, parts = refs[count:]
    tiles, span, per, _, _ = blocks[0].shape
    excess = tree_sum([partial[0] for partial in partials])
    error = tree_sum([partial[1] for partial in partials])
    weights = excess / (error * error)
    rows = weighted.shape[0]
    for v in range(count):
        parts[v] = weights[v * rows : (v + 1) * rows]
    weighted[...] = parts[pos[0]]
    rounded = high_part(weights)
    for b in range(per):
        spare[pl.ds(b, tiles, stride=per), :] = rounded
    lefts = [spread_rows(spare[h * GROUP : (h + 1) * GROUP, :]) for h in range(tiles * per // GROUP)]
    for n, block in enumerate(blocks):

        @pl.when(pos[0] >= 0)
        def _():
            for u in range(span):
                i = n * span + u
                for h, left in enumerate(lefts):
                    right = jnp.concatenate(
                        [block[(h * GROUP + r) // per, u, r % per] for r in range(GROUP)], axis=0
                    )
                    sent = jnp.dot(left, right, preferred_element_type=F32)
                    rows = pl.ds(h * GROUP, GROUP)
                    out[i, rows, :] = (scale[half * out.shape[0] + i, rows, :] * sent).astype(BF16)


def scatter_half(count, pitch, half, pos, cols, sent, adjoint, flipped):
    some, picks, _ = sent[0].shape
    levels = cols[0].shape[1]
    tiles = pitch - 8
    tile = lax.broadcasted_iota(jnp.int32, (tiles, picks), 0)
    for k in range(count):
        flipped[k] = cols[k][...].T

    @pl.when(pos[0] >= 0)
    def _():
        for k in range(count):
            base = ((pos[0] ^ k) * levels + half * some) * pitch
            for i in range(some):
                hot = jnp.where(flipped[k, half * some + i, :][None, :] == tile, 1.0, 0.0).astype(BF16)
                total = jnp.dot(hot, sent[k][i], preferred_element_type=F32)
                adjoint[pl.ds(pl.multiple_of(base + i * pitch, 8), tiles), :] = total


def scatter_kernel(count, pitch, pos, *refs):
    scatter_half(count, pitch, 0, pos, refs[:count], refs[count : 2 * count], *refs[2 * count :])


def gradient_kernel(count, pitch, pos, root, chi, *refs):
    cols, sent = refs[:count], refs[count : 2 * count]
    _, out_hbm, adjoint, turned, flipped, out, written = refs[2 * count :]
    levels, width = chi.shape[0], sent[0].shape[2]
    tiles = chi.shape[1] // width
    every = root.shape[0]
    turned[...] = root[...].T
    scatter_half(count, pitch, 1, pos, cols, sent, adjoint, flipped)
    own = turned[pl.ds(pl.multiple_of(pos[0] * levels, 8), levels), :]
    own_high = high_part(own)
    own_low = own - own_high
    left = jnp.concatenate(
        [jnp.concatenate([own_high, own_high], axis=1), jnp.concatenate([own_low, own_low], axis=1)], axis=0
    ).astype(BF16)
    step = GRAD_STEP

    def put(i):
        part = pl.ds(pl.multiple_of(i * step * width, step * width), step * width)
        return pltpu.make_async_copy(out.at[:, part], out_hbm.at[:, part], written.at[i])

    @pl.loop(0, tiles // step)
    def _(i):
        for u in range(step):
            c = i * step + u
            rows = adjoint[pl.ds(c, every, stride=pitch), :]
            first = high_part(rows)
            right = jnp.concatenate([first, rows - first], axis=0).astype(BF16)
            both = jnp.dot(left, right, preferred_element_type=F32)
            part = pl.ds(pl.multiple_of(c * width, width), width)
            out[:, part] = chi[:, part] + (both[:levels] + both[levels:])
        put(i).start()

    for i in range(tiles // step):
        put(i).wait()


def exchange(x, axis, size, k):
    return lax.ppermute(x, axis, [(i, i ^ k) for i in range(size)])


def local(chi, bg_std, vert_root, obs_blocks, block_cols, departures, obs_std, obs_target):
    own_tiles, levels, per, width, _ = obs_blocks.shape
    cell_count = chi.shape[1]
    tiles = cell_count // width
    every = vert_root.shape[0]
    slot_rows = departures.shape[0]
    picks = own_tiles * per
    horiz = lax.axis_size("horiz")
    vert = lax.axis_size("vert")
    vert_pos = lax.axis_index("vert").astype(jnp.int32)
    horiz_pos = lax.axis_index("horiz").astype(jnp.int32)
    pitch = tiles + 8
    pos = jnp.stack([vert_pos, horiz_pos * (vert * slot_rows), horiz_pos * tiles])

    slot_shape = (slot_rows // width, width)

    def entries_shape(n):
        return jax.ShapeDtypeStruct((n, 3, *slot_shape), F32)

    cols, entries = call(
        pack_kernel,
        (jax.ShapeDtypeStruct((picks, levels), jnp.int32), entries_shape(1)),
        (
            pos,
            jnp.transpose(block_cols, (0, 2, 1)),
            departures.reshape(slot_shape),
            obs_std.reshape(slot_shape),
            obs_target.reshape(slot_shape),
        ),
        [
            pltpu.VMEM((own_tiles, per, levels), jnp.int32),
            pltpu.VMEM(slot_shape, jnp.int32),
            pltpu.SemaphoreType.DMA((4,)),
        ],
        left=(1, 2, 3, 4),
    )
    received = exchange(entries, "horiz", horiz, 1)
    all_cols = [cols] + [exchange(cols, "vert", vert, k) for k in range(1, vert)]

    part = jax.ShapeDtypeStruct((own_tiles, levels // PARTS, *obs_blocks.shape[2:]), BF16)
    pos, cols, entries = lax.optimization_barrier((pos, cols, entries))
    high, low, bg, *first_blocks = call(
        functools.partial(mix_kernel, levels, pitch),
        (
            jax.ShapeDtypeStruct((every * tiles, width), BF16),
            jax.ShapeDtypeStruct((levels * tiles, width), BF16),
            jax.ShapeDtypeStruct(bg_std.shape, F32),
        )
        + (part,) * IN_MIX,
        (pos, vert_root, chi, bg_std, obs_blocks),
        [
            pltpu.VMEM((every * pitch, width), F32),
            pltpu.VMEM(vert_root.shape, F32),
            pltpu.VMEM(chi.shape, F32),
            pltpu.SemaphoreType.DMA((tiles // MIX_STEP + 1,)),
            pltpu.SemaphoreType.DMA,
            pltpu.SemaphoreType.DMA((IN_MIX * SPLIT,)),
        ],
        left=(1, 2, 3, 4),
        mib=12,
    )
    picked_shape = (levels, picks, width)
    own_picks, joined, *sent_picks = call(
        functools.partial(pick_kernel, vert),
        (jax.ShapeDtypeStruct(picked_shape, F32), entries_shape(2))
        + (jax.ShapeDtypeStruct(picked_shape, BF16),) * (vert - 1)
        + (part,) * IN_PICK,
        (
            pos,
            *all_cols,
            high,
            low,
            entries,
            received,
            obs_blocks,
        ),
        [pltpu.SemaphoreType.DMA((IN_PICK * SPLIT,))],
        left=(5 + vert,),
    )
    second_blocks = sent_picks[vert - 1 :]
    got_picks = [exchange(sent_picks[k - 1], "vert", vert, k) for k in range(1, vert)]
    groups = [joined] + [exchange(joined, "horiz", horiz, k) for k in range(2, horiz, 2)]
    scale, *third_blocks = call(
        functools.partial(scale_kernel, pitch),
        (
            jax.ShapeDtypeStruct(picked_shape, F32),
        )
        + (part,) * IN_SCALE,
        (pos, cols, bg, obs_blocks),
        [pltpu.VMEM((levels * pitch, width), F32), pltpu.SemaphoreType.DMA((IN_SCALE * SPLIT,))],
        left=(3,),
        mib=6,
    )
    blocks = [*first_blocks, *second_blocks, *third_blocks]
    rest = PARTS - len(blocks)
    (placed,) = call(
        functools.partial(place_kernel, own_tiles),
        (jax.ShapeDtypeStruct((2, own_tiles, width), F32),),
        (pos, *groups),
    )
    partial, *last_blocks = call(
        functools.partial(forward_kernel, vert),
        (jax.ShapeDtypeStruct((2, own_tiles, width), F32),) + (part,) * rest,
        (pos, placed, scale, own_picks, *got_picks, *blocks, obs_blocks),
        [pltpu.VMEM((picks, width), F32), pltpu.SemaphoreType.DMA((rest * SPLIT,))],
        left=(3 + vert + len(blocks),),
    )
    blocks = [*blocks, *last_blocks]
    partials = [partial] + [exchange(partial, "vert", vert, k) for k in range(1, vert)]
    half_shape = (levels // 2, picks, width)
    sent = []
    for h in range(2):
        weighted, values = call(
            functools.partial(backward_kernel, vert, h),
            (jax.ShapeDtypeStruct(slot_shape, F32), jax.ShapeDtypeStruct(half_shape, BF16)),
            (pos, *partials, scale, *blocks[h * PARTS // 2 : (h + 1) * PARTS // 2]),
            [pltpu.VMEM((picks, width), F32), pltpu.VMEM((vert, *slot_shape), F32)],
        )
        sent.append([values] + [exchange(values, "vert", vert, k) for k in range(1, vert)])
    adjoint_shape = jax.ShapeDtypeStruct((every * pitch, width), F32)
    flipped = pltpu.VMEM((vert, levels, picks), jnp.int32)
    (adjoint,) = call(
        functools.partial(scatter_kernel, vert, pitch),
        (adjoint_shape,),
        (pos, *all_cols, *sent[0]),
        [flipped],
    )
    gradient, _ = call(
        functools.partial(gradient_kernel, vert, pitch),
        (jax.ShapeDtypeStruct(chi.shape, F32), adjoint_shape),
        (pos, vert_root, chi, *all_cols, *sent[1], adjoint),
        [
            pltpu.VMEM((every, every), F32),
            flipped,
            pltpu.VMEM(chi.shape, F32),
            pltpu.SemaphoreType.DMA((tiles // GRAD_STEP,)),
        ],
        mib=6,
        outside=(0,),
        aliases={3 + 2 * vert: 1},
    )
    return gradient, weighted.reshape(slot_rows)


def solution(mesh):
    in_specs = (
        P("vert", "horiz"),
        P("vert", "horiz"),
        P(),
        P("horiz", "vert", None, None, None),
        P("horiz", "vert", None),
        P(("horiz", "vert")),
        P(("horiz", "vert")),
        P(("horiz", "vert")),
    )
    out_specs = (P("vert", "horiz"), P(("horiz", "vert")))
    return jax.shard_map(local, mesh=mesh, in_specs=in_specs, out_specs=out_specs, check_vma=False)
```

```python
import functools

import jax
import jax.numpy as jnp
from jax import lax
from jax.experimental import pallas as pl
from jax.experimental.pallas import tpu as pltpu
from jax.sharding import PartitionSpec as P

F32 = jnp.float32
BF16 = jnp.bfloat16
GROUP = 16
MIX_STEP = 32
SCALE_STEP = 32
GRAD_STEP = 32
PARTS = 8
SPLIT = 4
IN_MIX = 2
IN_PICK = 1
IN_SCALE = 2
VECTOR_TILES = 8
CUT = 4
VMEM = pl.BlockSpec(memory_space=pltpu.VMEM)
SMEM = pl.BlockSpec(memory_space=pltpu.SMEM)
HBM = pl.BlockSpec(memory_space=pl.ANY)


def call(body, outs, inputs, scratch=(), mib=2, left=(), outside=(), aliases=None):
    inputs = [
        x if i == 0 else pltpu.with_memory_space_constraint(x, pltpu.HBM if i in left else pltpu.VMEM)
        for i, x in enumerate(inputs)
    ]
    outs = [x if n in outside else pltpu.VMEM(x.shape, x.dtype) for n, x in enumerate(outs)]
    return pl.pallas_call(
        body,
        out_shape=outs,
        in_specs=[SMEM] + [HBM if i in left else VMEM for i in range(1, len(inputs))],
        out_specs=[HBM if n in outside else VMEM for n in range(len(outs))],
        scratch_shapes=list(scratch),
        input_output_aliases=aliases or {},
        compiler_params=pltpu.CompilerParams(vmem_limit_bytes=mib << 20),
        cost_estimate=pl.CostEstimate(flops=1024, bytes_accessed=1024, transcendentals=0),
    )(*inputs)


def high_part(x):
    return x.astype(BF16).astype(F32)


def nt_dot(a, b):
    return lax.dot_general(a, b, (((1,), (1,)), ((), ())), preferred_element_type=F32)


def spread_rows(x):
    row = lax.broadcasted_iota(jnp.int32, x.shape, 0)
    return jnp.concatenate([jnp.where(row == r, x, 0.0).astype(BF16) for r in range(GROUP)], axis=1)


def tree_sum(values):
    while len(values) > 1:
        values = [values[i] + values[i + 1] for i in range(0, len(values), 2)]
    return values[0]


def block_copies(source, parts, first, arrived):
    rows = parts[0].shape[0] // SPLIT
    span = parts[0].shape[1]
    copies = []
    for n, part in enumerate(parts):
        for m in range(SPLIT):
            piece = pl.ds(m * rows, rows)
            there = source.at[piece, pl.ds((first + n) * span, span)]
            copies.append(pltpu.make_async_copy(there, part.at[piece], arrived.at[n * SPLIT + m]))
    return copies


def pack_kernel(pos, table_hbm, value_hbm, error_hbm, target_hbm, cols, entries, table, target, arrived):
    copies = [
        pltpu.make_async_copy(table_hbm, table, arrived.at[0]),
        pltpu.make_async_copy(value_hbm, entries.at[0, 0], arrived.at[1]),
        pltpu.make_async_copy(error_hbm, entries.at[0, 1], arrived.at[2]),
        pltpu.make_async_copy(target_hbm, target, arrived.at[3]),
    ]
    for copy in copies:
        copy.start()
    for copy in copies:
        copy.wait()
    per = table.shape[1]
    for t in range(table.shape[0]):
        cols[t * per : (t + 1) * per, :] = table[t] - pos[2]
    entries[0, 2] = target[...].astype(F32)


def mix_kernel(levels, pitch, pos, root_hbm, chi_hbm, bg_hbm, blocks_hbm, high, low, bg, *refs):
    *parts, mixed, root, chi, arrived, bg_arrived, blocks_arrived = refs
    every = root.shape[0]
    width = high.shape[1]
    tiles = chi.shape[1] // width
    step = MIX_STEP
    pieces = tiles // step

    def fetch(i):
        part = pl.ds(pl.multiple_of(i * step * width, step * width), step * width)
        return pltpu.make_async_copy(chi_hbm.at[:, part], chi.at[:, part], arrived.at[i])

    root_copy = pltpu.make_async_copy(root_hbm, root, arrived.at[pieces])
    root_copy.start()
    for i in range(pieces):
        fetch(i).start()
    copies = [pltpu.make_async_copy(bg_hbm, bg, bg_arrived)] + block_copies(blocks_hbm, parts, 0, blocks_arrived)
    root_copy.wait()
    lane = lax.broadcasted_iota(jnp.int32, root.shape, 1)
    table = root[...]
    left = jnp.zeros(root.shape, F32)
    for g in range(4):
        own = pltpu.roll(table, (g * levels - pos[0] * levels + every) % every, 1)
        own_high = high_part(own)
        part = own_high if g < 2 else own - own_high
        left = jnp.where(lane // levels == g, part, left)
    left = left[:, : 4 * levels].astype(BF16)

    @pl.loop(0, pieces)
    def _(i):
        fetch(i).wait()

        @pl.when(i == 0)
        def _():
            for copy in copies:
                copy.start()

        for u in range(step):
            c = i * step + u
            x = chi[:, pl.ds(pl.multiple_of(c * width, width), width)]
            x_high = high_part(x)
            x_low = x - x_high
            right = jnp.concatenate([x_high, x_low, x_high, x_low], axis=0).astype(BF16)
            mixed[pl.ds(c, every, stride=pitch), :] = jnp.dot(left, right, preferred_element_type=F32)

    @pl.loop(0, every // step)
    def _(i):
        for u in range(step):
            l = i * step + u
            rows = mixed[pl.ds(pl.multiple_of(l * pitch, 8), tiles), :]
            high[pl.ds(pl.multiple_of(l * tiles, tiles), tiles), :] = rows.astype(BF16)

    @pl.loop(0, levels)
    def _(i):
        rows = mixed[pl.ds(pl.multiple_of((pos[0] * levels + i) * pitch, 8), tiles), :]
        low[pl.ds(pl.multiple_of(i * tiles, tiles), tiles), :] = (rows - high_part(rows)).astype(BF16)

    for copy in copies:
        copy.wait()


def pick_kernel(count, pos, *refs):
    cols = refs[:count]
    high, low, entries, received, blocks_hbm, own, joined = refs[count : count + 7]
    *outs, block_arrived = refs[count + 7 :]
    copies = block_copies(blocks_hbm, outs[count - 1 :], IN_MIX, block_arrived)
    for copy in copies:
        copy.start()
    joined[:1] = entries[...]
    joined[1:] = received[...]
    levels = cols[0].shape[1]
    tiles = low.shape[0] // levels
    tile = lax.broadcasted_iota(jnp.int32, (cols[0].shape[0], tiles), 1)

    @pl.when(pos[0] >= 0)
    def _():
        for k in range(count):
            wanted = cols[k][...]
            base = (pos[0] ^ k) * levels * tiles
            for i in range(levels):
                hot = jnp.where(wanted[:, i : i + 1] == tile, 1.0, 0.0).astype(BF16)
                rows = high[pl.ds(pl.multiple_of(base + i * tiles, tiles), tiles), :]
                picked = jnp.dot(hot, rows, preferred_element_type=F32)
                if k == 0:
                    rows = low[i * tiles : (i + 1) * tiles, :]
                    own[i] = picked + jnp.dot(hot, rows, preferred_element_type=F32)
                else:
                    outs[k - 1][i] = picked.astype(BF16)

    for copy in copies:
        copy.wait()


def scale_kernel(pitch, pos, cols, bg, blocks_hbm, out, *refs):
    *parts, spaced, block_arrived = refs
    copies = block_copies(blocks_hbm, parts, IN_MIX + IN_PICK, block_arrived)
    for copy in copies:
        copy.start()
    levels, width = bg.shape[0], out.shape[2]
    tiles = bg.shape[1] // width
    step = SCALE_STEP

    @pl.loop(0, tiles // step)
    def _(i):
        for u in range(step):
            c = i * step + u
            spaced[pl.ds(c, levels, stride=pitch), :] = bg[:, pl.ds(pl.multiple_of(c * width, width), width)]

    tile = lax.broadcasted_iota(jnp.int32, (cols.shape[0], tiles), 1)
    wanted = cols[...]
    for i in range(levels):
        hot = jnp.where(wanted[:, i : i + 1] == tile, 1.0, 0.0).astype(BF16)
        rows = spaced[i * pitch : i * pitch + tiles, :]
        first = high_part(rows)
        second = high_part(rows - first)
        third = rows - first - second
        parts = jnp.concatenate([first, second, third], axis=1).astype(BF16)
        picked = jnp.dot(hot, parts, preferred_element_type=F32)
        out[i] = picked[:, :width] + picked[:, width : 2 * width] + picked[:, 2 * width :]
    for copy in copies:
        copy.wait()


def place_kernel(rows, pos, *refs):
    *groups, out = refs
    width = out.shape[2]
    index = lax.broadcasted_iota(jnp.int32, (6 * rows, width), 0)
    term, slot = index // rows, index % rows
    place = lax.broadcasted_iota(jnp.int32, (width, width), 0)
    total = jnp.zeros((6 * rows, width), F32)
    for entry in [group.at[n] for group in groups for n in range(group.shape[0])]:
        for e in range(entry.shape[1]):
            target = entry[2, e : e + 1, :].astype(jnp.int32) - pos[1]
            left = jnp.zeros((6 * rows, width), F32)
            for which in range(2):
                value = entry[which, e : e + 1, :]
                first = high_part(value)
                second = high_part(value - first)
                for m, part in enumerate((first, second, value - first - second)):
                    left = jnp.where(term == 3 * which + m, part, left)
            left = jnp.where(slot == target // width, left, 0.0).astype(BF16)
            hot = jnp.where(target % width == place, 1.0, 0.0).astype(BF16)
            total += nt_dot(left, hot)
    for which in range(2):
        base = 3 * which * rows
        out[which] = total[base : base + rows] + total[base + rows : base + 2 * rows] + total[base + 2 * rows : base + 3 * rows]


def forward_kernel(count, pos, placed, scale, own, *refs):
    others, refs = refs[: count - 1], refs[count - 1 :]
    held = IN_MIX + IN_PICK + IN_SCALE
    early, (blocks_hbm, out, *late) = refs[:held], refs[held:-4]
    spare, lines, sums, arrived = refs[-4:]
    copies = block_copies(blocks_hbm, late, held, arrived)
    for copy in copies:
        copy.start()
    tiles, span, per, width, _ = early[0].shape
    start = tiles - VECTOR_TILES
    groups = start * per // GROUP
    spare[...] = jnp.zeros_like(spare)
    for n, part in enumerate((*early, *late)):
        for copy in copies[max(n - held, 0) * SPLIT : max(n - held + 1, 0) * SPLIT]:
            copy.wait()

        @pl.when(pos[0] >= 0)
        def _():
            totals = [spare[h * GROUP : (h + 1) * GROUP, :] for h in range(groups)]
            lefts = []
            for u in range(span):
                l = n * span + u
                mixed = own[l]
                for other in others:
                    mixed = mixed + other[l].astype(F32)
                values = high_part(scale[l] * mixed)
                lines[u] = values[groups * GROUP :]
                lefts.append([spread_rows(values[h * GROUP : (h + 1) * GROUP]) for h in range(groups)])
            cuts = GROUP // CUT
            tasks = [(u, h, q) for u in range(span) for h in range(groups) for q in range(cuts)]
            turns = VECTOR_TILES * span
            for t in range(VECTOR_TILES):
                total = jnp.zeros((width, width), F32) if n == 0 else sums[t]
                for v in range(span):
                    turn = t * span + v
                    for u, h, q in tasks[turn * len(tasks) // turns : (turn + 1) * len(tasks) // turns]:
                        right = jnp.concatenate(
                            [part[(h * GROUP + r) // per, u, r % per] for r in range(q * CUT, (q + 1) * CUT)], axis=1
                        )
                        left = lefts[u][h][:, q * CUT * width : (q + 1) * CUT * width]
                        totals[h] = totals[h] + nt_dot(left, right)
                    for b in range(per):
                        line = lines[v, t * per + b : t * per + b + 1, :]
                        total = total + part[start + t, v, b].astype(F32) * line
                sums[t] = total
            for h, total in enumerate(totals):
                spare[h * GROUP : (h + 1) * GROUP, :] = total

    total = spare[pl.ds(0, start, stride=per), :]
    for b in range(1, per):
        total = total + spare[pl.ds(b, start, stride=per), :]
    ones = jnp.ones((8, width), BF16)
    reduced = [total]
    for t in range(VECTOR_TILES):
        first = high_part(sums[t])
        second = high_part(sums[t] - first)
        third = sums[t] - first - second
        row = nt_dot(ones, first.astype(BF16)) + nt_dot(ones, second.astype(BF16)) + nt_dot(ones, third.astype(BF16))
        reduced.append(row[:1])
    out[0] = jnp.concatenate(reduced, axis=0) - placed[0]
    out[1] = placed[1]


def backward_kernel(count, half, pos, *refs):
    partials = refs[:count]
    scale, *blocks, weighted, out, spare, parts = refs[count:]
    tiles, span, per, _, _ = blocks[0].shape
    excess = tree_sum([partial[0] for partial in partials])
    error = tree_sum([partial[1] for partial in partials])
    weights = excess / (error * error)
    rows = weighted.shape[0]
    for v in range(count):
        parts[v] = weights[v * rows : (v + 1) * rows]
    weighted[...] = parts[pos[0]]
    rounded = high_part(weights)
    for b in range(per):
        spare[pl.ds(b, tiles, stride=per), :] = rounded
    lefts = [spread_rows(spare[h * GROUP : (h + 1) * GROUP, :]) for h in range(tiles * per // GROUP)]
    for n, block in enumerate(blocks):

        @pl.when(pos[0] >= 0)
        def _():
            for u in range(span):
                i = n * span + u
                for h, left in enumerate(lefts):
                    right = jnp.concatenate(
                        [block[(h * GROUP + r) // per, u, r % per] for r in range(GROUP)], axis=0
                    )
                    sent = jnp.dot(left, right, preferred_element_type=F32)
                    rows = pl.ds(h * GROUP, GROUP)
                    out[i, rows, :] = (scale[half * out.shape[0] + i, rows, :] * sent).astype(BF16)


def scatter_half(count, pitch, half, pos, cols, sent, adjoint, flipped):
    some, picks, _ = sent[0].shape
    levels = cols[0].shape[1]
    tiles = pitch - 8
    tile = lax.broadcasted_iota(jnp.int32, (tiles, picks), 0)
    for k in range(count):
        flipped[k] = cols[k][...].T

    @pl.when(pos[0] >= 0)
    def _():
        for k in range(count):
            base = ((pos[0] ^ k) * levels + half * some) * pitch
            for i in range(some):
                hot = jnp.where(flipped[k, half * some + i, :][None, :] == tile, 1.0, 0.0).astype(BF16)
                total = jnp.dot(hot, sent[k][i], preferred_element_type=F32)
                adjoint[pl.ds(pl.multiple_of(base + i * pitch, 8), tiles), :] = total


def scatter_kernel(count, pitch, pos, *refs):
    scatter_half(count, pitch, 0, pos, refs[:count], refs[count : 2 * count], *refs[2 * count :])


def gradient_kernel(count, pitch, pos, root, chi, *refs):
    cols, sent = refs[:count], refs[count : 2 * count]
    _, out_hbm, adjoint, turned, flipped, out, written = refs[2 * count :]
    levels, width = chi.shape[0], sent[0].shape[2]
    tiles = chi.shape[1] // width
    every = root.shape[0]
    turned[...] = root[...].T
    scatter_half(count, pitch, 1, pos, cols, sent, adjoint, flipped)
    own = turned[pl.ds(pl.multiple_of(pos[0] * levels, 8), levels), :]
    own_high = high_part(own)
    own_low = own - own_high
    left = jnp.concatenate(
        [jnp.concatenate([own_high, own_high], axis=1), jnp.concatenate([own_low, own_low], axis=1)], axis=0
    ).astype(BF16)
    step = GRAD_STEP

    def put(i):
        part = pl.ds(pl.multiple_of(i * step * width, step * width), step * width)
        return pltpu.make_async_copy(out.at[:, part], out_hbm.at[:, part], written.at[i])

    @pl.loop(0, tiles // step)
    def _(i):
        for u in range(step):
            c = i * step + u
            rows = adjoint[pl.ds(c, every, stride=pitch), :]
            first = high_part(rows)
            right = jnp.concatenate([first, rows - first], axis=0).astype(BF16)
            both = jnp.dot(left, right, preferred_element_type=F32)
            part = pl.ds(pl.multiple_of(c * width, width), width)
            out[:, part] = chi[:, part] + (both[:levels] + both[levels:])
        put(i).start()

    for i in range(tiles // step):
        put(i).wait()


def exchange(x, axis, size, k):
    return lax.ppermute(x, axis, [(i, i ^ k) for i in range(size)])


def local(chi, bg_std, vert_root, obs_blocks, block_cols, departures, obs_std, obs_target):
    own_tiles, levels, per, width, _ = obs_blocks.shape
    cell_count = chi.shape[1]
    tiles = cell_count // width
    every = vert_root.shape[0]
    slot_rows = departures.shape[0]
    picks = own_tiles * per
    horiz = lax.axis_size("horiz")
    vert = lax.axis_size("vert")
    vert_pos = lax.axis_index("vert").astype(jnp.int32)
    horiz_pos = lax.axis_index("horiz").astype(jnp.int32)
    pitch = tiles + 8
    pos = jnp.stack([vert_pos, horiz_pos * (vert * slot_rows), horiz_pos * tiles])

    slot_shape = (slot_rows // width, width)

    def entries_shape(n):
        return jax.ShapeDtypeStruct((n, 3, *slot_shape), F32)

    cols, entries = call(
        pack_kernel,
        (jax.ShapeDtypeStruct((picks, levels), jnp.int32), entries_shape(1)),
        (
            pos,
            jnp.transpose(block_cols, (0, 2, 1)),
            departures.reshape(slot_shape),
            obs_std.reshape(slot_shape),
            obs_target.reshape(slot_shape),
        ),
        [
            pltpu.VMEM((own_tiles, per, levels), jnp.int32),
            pltpu.VMEM(slot_shape, jnp.int32),
            pltpu.SemaphoreType.DMA((4,)),
        ],
        left=(1, 2, 3, 4),
    )
    received = exchange(entries, "horiz", horiz, 1)
    all_cols = [cols] + [exchange(cols, "vert", vert, k) for k in range(1, vert)]

    part = jax.ShapeDtypeStruct((own_tiles, levels // PARTS, *obs_blocks.shape[2:]), BF16)
    pos, cols, entries = lax.optimization_barrier((pos, cols, entries))
    high, low, bg, *first_blocks = call(
        functools.partial(mix_kernel, levels, pitch),
        (
            jax.ShapeDtypeStruct((every * tiles, width), BF16),
            jax.ShapeDtypeStruct((levels * tiles, width), BF16),
            jax.ShapeDtypeStruct(bg_std.shape, F32),
        )
        + (part,) * IN_MIX,
        (pos, vert_root, chi, bg_std, obs_blocks),
        [
            pltpu.VMEM((every * pitch, width), F32),
            pltpu.VMEM(vert_root.shape, F32),
            pltpu.VMEM(chi.shape, F32),
            pltpu.SemaphoreType.DMA((tiles // MIX_STEP + 1,)),
            pltpu.SemaphoreType.DMA,
            pltpu.SemaphoreType.DMA((IN_MIX * SPLIT,)),
        ],
        left=(1, 2, 3, 4),
        mib=12,
    )
    picked_shape = (levels, picks, width)
    own_picks, joined, *sent_picks = call(
        functools.partial(pick_kernel, vert),
        (jax.ShapeDtypeStruct(picked_shape, F32), entries_shape(2))
        + (jax.ShapeDtypeStruct(picked_shape, BF16),) * (vert - 1)
        + (part,) * IN_PICK,
        (
            pos,
            *all_cols,
            high,
            low,
            entries,
            received,
            obs_blocks,
        ),
        [pltpu.SemaphoreType.DMA((IN_PICK * SPLIT,))],
        left=(5 + vert,),
    )
    second_blocks = sent_picks[vert - 1 :]
    got_picks = [exchange(sent_picks[k - 1], "vert", vert, k) for k in range(1, vert)]
    groups = [joined] + [exchange(joined, "horiz", horiz, k) for k in range(2, horiz, 2)]
    scale, *third_blocks = call(
        functools.partial(scale_kernel, pitch),
        (
            jax.ShapeDtypeStruct(picked_shape, F32),
        )
        + (part,) * IN_SCALE,
        (pos, cols, bg, obs_blocks),
        [pltpu.VMEM((levels * pitch, width), F32), pltpu.SemaphoreType.DMA((IN_SCALE * SPLIT,))],
        left=(3,),
        mib=6,
    )
    blocks = [*first_blocks, *second_blocks, *third_blocks]
    rest = PARTS - len(blocks)
    (placed,) = call(
        functools.partial(place_kernel, own_tiles),
        (jax.ShapeDtypeStruct((2, own_tiles, width), F32),),
        (pos, *groups),
    )
    partial, *last_blocks = call(
        functools.partial(forward_kernel, vert),
        (jax.ShapeDtypeStruct((2, own_tiles, width), F32),) + (part,) * rest,
        (pos, placed, scale, own_picks, *got_picks, *blocks, obs_blocks),
        [
            pltpu.VMEM((picks - VECTOR_TILES * per, width), F32),
            pltpu.VMEM((levels // PARTS, VECTOR_TILES * per, width), F32),
            pltpu.VMEM((VECTOR_TILES, width, width), F32),
            pltpu.SemaphoreType.DMA((rest * SPLIT,)),
        ],
        left=(3 + vert + len(blocks),),
    )
    blocks = [*blocks, *last_blocks]
    partials = [partial] + [exchange(partial, "vert", vert, k) for k in range(1, vert)]
    half_shape = (levels // 2, picks, width)
    sent = []
    for h in range(2):
        weighted, values = call(
            functools.partial(backward_kernel, vert, h),
            (jax.ShapeDtypeStruct(slot_shape, F32), jax.ShapeDtypeStruct(half_shape, BF16)),
            (pos, *partials, scale, *blocks[h * PARTS // 2 : (h + 1) * PARTS // 2]),
            [pltpu.VMEM((picks, width), F32), pltpu.VMEM((vert, *slot_shape), F32)],
        )
        sent.append([values] + [exchange(values, "vert", vert, k) for k in range(1, vert)])
    adjoint_shape = jax.ShapeDtypeStruct((every * pitch, width), F32)
    flipped = pltpu.VMEM((vert, levels, picks), jnp.int32)
    (adjoint,) = call(
        functools.partial(scatter_kernel, vert, pitch),
        (adjoint_shape,),
        (pos, *all_cols, *sent[0]),
        [flipped],
    )
    gradient, _ = call(
        functools.partial(gradient_kernel, vert, pitch),
        (jax.ShapeDtypeStruct(chi.shape, F32), adjoint_shape),
        (pos, vert_root, chi, *all_cols, *sent[1], adjoint),
        [
            pltpu.VMEM((every, every), F32),
            flipped,
            pltpu.VMEM(chi.shape, F32),
            pltpu.SemaphoreType.DMA((tiles // GRAD_STEP,)),
        ],
        mib=6,
        outside=(0,),
        aliases={3 + 2 * vert: 1},
    )
    return gradient, weighted.reshape(slot_rows)


def solution(mesh):
    in_specs = (
        P("vert", "horiz"),
        P("vert", "horiz"),
        P(),
        P("horiz", "vert", None, None, None),
        P("horiz", "vert", None),
        P(("horiz", "vert")),
        P(("horiz", "vert")),
        P(("horiz", "vert")),
    )
    out_specs = (P("vert", "horiz"), P(("horiz", "vert")))
    return jax.shard_map(local, mesh=mesh, in_specs=in_specs, out_specs=out_specs, check_vma=False)
```

```python
import functools

import jax
import jax.numpy as jnp
from jax import lax
from jax.experimental import pallas as pl
from jax.experimental.pallas import tpu as pltpu
from jax.sharding import PartitionSpec as P

F32 = jnp.float32
BF16 = jnp.bfloat16
GROUP = 16
MIX_STEP = 32
SCALE_STEP = 32
GRAD_STEP = 32
PARTS = 8
SPLIT = 4
IN_MIX = 1
IN_PICK = 1
IN_SCALE = 2
VECTOR_TILES = 8
CUT = 4
VMEM = pl.BlockSpec(memory_space=pltpu.VMEM)
SMEM = pl.BlockSpec(memory_space=pltpu.SMEM)
HBM = pl.BlockSpec(memory_space=pl.ANY)


def call(body, outs, inputs, scratch=(), mib=2, left=(), outside=(), aliases=None):
    inputs = [
        x if i == 0 else pltpu.with_memory_space_constraint(x, pltpu.HBM if i in left else pltpu.VMEM)
        for i, x in enumerate(inputs)
    ]
    outs = [x if n in outside else pltpu.VMEM(x.shape, x.dtype) for n, x in enumerate(outs)]
    return pl.pallas_call(
        body,
        out_shape=outs,
        in_specs=[SMEM] + [HBM if i in left else VMEM for i in range(1, len(inputs))],
        out_specs=[HBM if n in outside else VMEM for n in range(len(outs))],
        scratch_shapes=list(scratch),
        input_output_aliases=aliases or {},
        compiler_params=pltpu.CompilerParams(vmem_limit_bytes=mib << 20),
        cost_estimate=pl.CostEstimate(flops=1024, bytes_accessed=1024, transcendentals=0),
    )(*inputs)


def high_part(x):
    return x.astype(BF16).astype(F32)


def nt_dot(a, b):
    return lax.dot_general(a, b, (((1,), (1,)), ((), ())), preferred_element_type=F32)


def spread_rows(x):
    row = lax.broadcasted_iota(jnp.int32, x.shape, 0)
    return jnp.concatenate([jnp.where(row == r, x, 0.0).astype(BF16) for r in range(GROUP)], axis=1)


def tree_sum(values):
    while len(values) > 1:
        values = [values[i] + values[i + 1] for i in range(0, len(values), 2)]
    return values[0]


def block_copies(source, parts, first, arrived):
    rows = parts[0].shape[0] // SPLIT
    span = parts[0].shape[1]
    copies = []
    for n, part in enumerate(parts):
        for m in range(SPLIT):
            piece = pl.ds(m * rows, rows)
            there = source.at[piece, pl.ds((first + n) * span, span)]
            copies.append(pltpu.make_async_copy(there, part.at[piece], arrived.at[n * SPLIT + m]))
    return copies


def pack_kernel(pos, table_hbm, value_hbm, error_hbm, target_hbm, cols, entries, table, target, arrived):
    copies = [
        pltpu.make_async_copy(table_hbm, table, arrived.at[0]),
        pltpu.make_async_copy(value_hbm, entries.at[0, 0], arrived.at[1]),
        pltpu.make_async_copy(error_hbm, entries.at[0, 1], arrived.at[2]),
        pltpu.make_async_copy(target_hbm, target, arrived.at[3]),
    ]
    for copy in copies:
        copy.start()
    for copy in copies:
        copy.wait()
    per = table.shape[1]
    for t in range(table.shape[0]):
        cols[t * per : (t + 1) * per, :] = table[t] - pos[2]
    entries[0, 2] = target[...].astype(F32)


def mix_kernel(levels, pitch, pos, root_hbm, chi_hbm, bg_hbm, blocks_hbm, high, low, bg, *refs):
    *parts, mixed, root, chi, arrived, bg_arrived, blocks_arrived = refs
    every = root.shape[0]
    width = high.shape[1]
    tiles = chi.shape[1] // width
    step = MIX_STEP
    pieces = tiles // step

    def fetch(i):
        part = pl.ds(pl.multiple_of(i * step * width, step * width), step * width)
        return pltpu.make_async_copy(chi_hbm.at[:, part], chi.at[:, part], arrived.at[i])

    root_copy = pltpu.make_async_copy(root_hbm, root, arrived.at[pieces])
    root_copy.start()
    for i in range(pieces):
        fetch(i).start()
    copies = [pltpu.make_async_copy(bg_hbm, bg, bg_arrived)] + block_copies(blocks_hbm, parts, 0, blocks_arrived)
    root_copy.wait()
    lane = lax.broadcasted_iota(jnp.int32, root.shape, 1)
    table = root[...]
    left = jnp.zeros(root.shape, F32)
    for g in range(4):
        own = pltpu.roll(table, (g * levels - pos[0] * levels + every) % every, 1)
        own_high = high_part(own)
        part = own_high if g < 2 else own - own_high
        left = jnp.where(lane // levels == g, part, left)
    left = left[:, : 4 * levels].astype(BF16)

    @pl.loop(0, pieces)
    def _(i):
        fetch(i).wait()

        @pl.when(i == 0)
        def _():
            for copy in copies:
                copy.start()

        for u in range(step):
            c = i * step + u
            x = chi[:, pl.ds(pl.multiple_of(c * width, width), width)]
            x_high = high_part(x)
            x_low = x - x_high
            right = jnp.concatenate([x_high, x_low, x_high, x_low], axis=0).astype(BF16)
            mixed[pl.ds(c, every, stride=pitch), :] = jnp.dot(left, right, preferred_element_type=F32)

    @pl.loop(0, every // step)
    def _(i):
        for u in range(step):
            l = i * step + u
            rows = mixed[pl.ds(pl.multiple_of(l * pitch, 8), tiles), :]
            high[pl.ds(pl.multiple_of(l * tiles, tiles), tiles), :] = rows.astype(BF16)

    @pl.loop(0, levels)
    def _(i):
        rows = mixed[pl.ds(pl.multiple_of((pos[0] * levels + i) * pitch, 8), tiles), :]
        low[pl.ds(pl.multiple_of(i * tiles, tiles), tiles), :] = (rows - high_part(rows)).astype(BF16)

    for copy in copies:
        copy.wait()


def pick_kernel(count, pos, *refs):
    cols = refs[:count]
    high, low, entries, received, blocks_hbm, own, joined = refs[count : count + 7]
    *outs, block_arrived = refs[count + 7 :]
    copies = block_copies(blocks_hbm, outs[count - 1 :], IN_MIX, block_arrived)
    for copy in copies:
        copy.start()
    joined[:1] = entries[...]
    joined[1:] = received[...]
    levels = cols[0].shape[1]
    tiles = low.shape[0] // levels
    tile = lax.broadcasted_iota(jnp.int32, (cols[0].shape[0], tiles), 1)

    @pl.when(pos[0] >= 0)
    def _():
        for k in range(count):
            wanted = cols[k][...]
            base = (pos[0] ^ k) * levels * tiles
            for i in range(levels):
                hot = jnp.where(wanted[:, i : i + 1] == tile, 1.0, 0.0).astype(BF16)
                rows = high[pl.ds(pl.multiple_of(base + i * tiles, tiles), tiles), :]
                picked = jnp.dot(hot, rows, preferred_element_type=F32)
                if k == 0:
                    rows = low[i * tiles : (i + 1) * tiles, :]
                    own[i] = picked + jnp.dot(hot, rows, preferred_element_type=F32)
                else:
                    outs[k - 1][i] = picked.astype(BF16)

    for copy in copies:
        copy.wait()


def scale_kernel(pitch, pos, cols, bg, blocks_hbm, out, *refs):
    *parts, spaced, block_arrived = refs
    copies = block_copies(blocks_hbm, parts, IN_MIX + IN_PICK, block_arrived)
    for copy in copies:
        copy.start()
    levels, width = bg.shape[0], out.shape[2]
    tiles = bg.shape[1] // width
    step = SCALE_STEP

    @pl.loop(0, tiles // step)
    def _(i):
        for u in range(step):
            c = i * step + u
            spaced[pl.ds(c, levels, stride=pitch), :] = bg[:, pl.ds(pl.multiple_of(c * width, width), width)]

    tile = lax.broadcasted_iota(jnp.int32, (cols.shape[0], tiles), 1)
    wanted = cols[...]
    for i in range(levels):
        hot = jnp.where(wanted[:, i : i + 1] == tile, 1.0, 0.0).astype(BF16)
        rows = spaced[i * pitch : i * pitch + tiles, :]
        first = high_part(rows)
        second = high_part(rows - first)
        third = rows - first - second
        parts = jnp.concatenate([first, second, third], axis=1).astype(BF16)
        picked = jnp.dot(hot, parts, preferred_element_type=F32)
        out[i] = picked[:, :width] + picked[:, width : 2 * width] + picked[:, 2 * width :]
    for copy in copies:
        copy.wait()


def place_kernel(rows, pos, *refs):
    *groups, out = refs
    width = out.shape[2]
    index = lax.broadcasted_iota(jnp.int32, (6 * rows, width), 0)
    term, slot = index // rows, index % rows
    place = lax.broadcasted_iota(jnp.int32, (width, width), 0)
    total = jnp.zeros((6 * rows, width), F32)
    for entry in [group.at[n] for group in groups for n in range(group.shape[0])]:
        for e in range(entry.shape[1]):
            target = entry[2, e : e + 1, :].astype(jnp.int32) - pos[1]
            left = jnp.zeros((6 * rows, width), F32)
            for which in range(2):
                value = entry[which, e : e + 1, :]
                first = high_part(value)
                second = high_part(value - first)
                for m, part in enumerate((first, second, value - first - second)):
                    left = jnp.where(term == 3 * which + m, part, left)
            left = jnp.where(slot == target // width, left, 0.0).astype(BF16)
            hot = jnp.where(target % width == place, 1.0, 0.0).astype(BF16)
            total += nt_dot(left, hot)
    for which in range(2):
        base = 3 * which * rows
        out[which] = total[base : base + rows] + total[base + rows : base + 2 * rows] + total[base + 2 * rows : base + 3 * rows]


def forward_kernel(count, pos, placed, scale, own, *refs):
    others, refs = refs[: count - 1], refs[count - 1 :]
    held = IN_MIX + IN_PICK + IN_SCALE
    early, (blocks_hbm, out, *late) = refs[:held], refs[held:-4]
    spare, lines, sums, arrived = refs[-4:]
    copies = block_copies(blocks_hbm, late, held, arrived)
    for copy in copies:
        copy.start()
    tiles, span, per, width, _ = early[0].shape
    start = tiles - VECTOR_TILES
    groups = start * per // GROUP
    spare[...] = jnp.zeros_like(spare)
    for n, part in enumerate((*early, *late)):
        for copy in copies[max(n - held, 0) * SPLIT : max(n - held + 1, 0) * SPLIT]:
            copy.wait()

        @pl.when(pos[0] >= 0)
        def _():
            totals = [spare[h * GROUP : (h + 1) * GROUP, :] for h in range(groups)]
            lefts = []
            for u in range(span):
                l = n * span + u
                mixed = own[l]
                for other in others:
                    mixed = mixed + other[l].astype(F32)
                values = high_part(scale[l] * mixed)
                lines[u] = values[groups * GROUP :]
                lefts.append([spread_rows(values[h * GROUP : (h + 1) * GROUP]) for h in range(groups)])
            cuts = GROUP // CUT
            tasks = [(u, h, q) for u in range(span) for h in range(groups) for q in range(cuts)]
            turns = VECTOR_TILES * span
            for t in range(VECTOR_TILES):
                total = jnp.zeros((width, width), F32) if n == 0 else sums[t]
                for v in range(span):
                    turn = t * span + v
                    for u, h, q in tasks[turn * len(tasks) // turns : (turn + 1) * len(tasks) // turns]:
                        right = jnp.concatenate(
                            [part[(h * GROUP + r) // per, u, r % per] for r in range(q * CUT, (q + 1) * CUT)], axis=1
                        )
                        left = lefts[u][h][:, q * CUT * width : (q + 1) * CUT * width]
                        totals[h] = totals[h] + nt_dot(left, right)
                    for b in range(per):
                        line = lines[v, t * per + b : t * per + b + 1, :]
                        total = total + part[start + t, v, b].astype(F32) * line
                sums[t] = total
            for h, total in enumerate(totals):
                spare[h * GROUP : (h + 1) * GROUP, :] = total

    total = spare[pl.ds(0, start, stride=per), :]
    for b in range(1, per):
        total = total + spare[pl.ds(b, start, stride=per), :]
    ones = jnp.ones((8, width), BF16)
    reduced = [total]
    for t in range(VECTOR_TILES):
        first = high_part(sums[t])
        second = high_part(sums[t] - first)
        third = sums[t] - first - second
        row = nt_dot(ones, first.astype(BF16)) + nt_dot(ones, second.astype(BF16)) + nt_dot(ones, third.astype(BF16))
        reduced.append(row[:1])
    out[0] = jnp.concatenate(reduced, axis=0) - placed[0]
    out[1] = placed[1]


def backward_kernel(count, half, pos, *refs):
    partials = refs[:count]
    scale, *blocks, weighted, out, spare, parts = refs[count:]
    tiles, span, per, _, _ = blocks[0].shape
    excess = tree_sum([partial[0] for partial in partials])
    error = tree_sum([partial[1] for partial in partials])
    weights = excess / (error * error)
    rows = weighted.shape[0]
    for v in range(count):
        parts[v] = weights[v * rows : (v + 1) * rows]
    weighted[...] = parts[pos[0]]
    rounded = high_part(weights)
    for b in range(per):
        spare[pl.ds(b, tiles, stride=per), :] = rounded
    lefts = [spread_rows(spare[h * GROUP : (h + 1) * GROUP, :]) for h in range(tiles * per // GROUP)]

    @pl.when(pos[0] >= 0)
    def _():
        for i in range(out.shape[0]):
            part, u = blocks[i // span], i % span
            for h, left in enumerate(lefts):
                right = jnp.concatenate([part[(h * GROUP + r) // per, u, r % per] for r in range(GROUP)], axis=0)
                sent = jnp.dot(left, right, preferred_element_type=F32)
                rows = pl.ds(h * GROUP, GROUP)
                out[i, rows, :] = (scale[half * out.shape[0] + i, rows, :] * sent).astype(BF16)


def scatter(count, pitch, pieces, pos, cols, sent, adjoint, flipped):
    some, picks, _ = sent[0].shape
    levels = cols[0].shape[1]
    tiles = pitch - 8
    tile = lax.broadcasted_iota(jnp.int32, (tiles, picks), 0)
    for k in range(count):
        flipped[k] = cols[k][...].T

    @pl.when(pos[0] >= 0)
    def _():
        for values, (k, half) in zip(sent, pieces):
            base = ((pos[0] ^ k) * levels + half * some) * pitch
            for i in range(some):
                hot = jnp.where(flipped[k, half * some + i, :][None, :] == tile, 1.0, 0.0).astype(BF16)
                total = jnp.dot(hot, values[i], preferred_element_type=F32)
                adjoint[pl.ds(pl.multiple_of(base + i * pitch, 8), tiles), :] = total


def scatter_kernel(count, pitch, pos, root, *refs):
    cols, sent = refs[:count], refs[count : 2 * count + 1]
    adjoint, mixing, turned, flipped = refs[2 * count + 1 :]
    levels = cols[0].shape[1]
    turned[...] = root[...].T
    own = turned[pl.ds(pl.multiple_of(pos[0] * levels, 8), levels), :]
    own_high = high_part(own)
    own_low = own - own_high
    mixing[...] = jnp.concatenate(
        [jnp.concatenate([own_high, own_high], axis=1), jnp.concatenate([own_low, own_low], axis=1)], axis=0
    )
    pieces = [(k, 0) for k in range(count)] + [(0, 1)]
    scatter(count, pitch, pieces, pos, cols, sent, adjoint, flipped)


def gradient_kernel(count, pitch, pos, mixing, chi, *refs):
    cols, sent = refs[:count], refs[count : 2 * count - 1]
    _, out_hbm, adjoint, flipped, out, written = refs[2 * count - 1 :]
    levels, width = chi.shape[0], sent[0].shape[2]
    tiles = chi.shape[1] // width
    every = mixing.shape[1] // 2
    pieces = [(k, 1) for k in range(1, count)]
    scatter(count, pitch, pieces, pos, cols, sent, adjoint, flipped)
    left = mixing[...].astype(BF16)
    step = GRAD_STEP

    def put(i):
        part = pl.ds(pl.multiple_of(i * step * width, step * width), step * width)
        return pltpu.make_async_copy(out.at[:, part], out_hbm.at[:, part], written.at[i])

    @pl.loop(0, tiles // step)
    def _(i):
        for u in range(step):
            c = i * step + u
            rows = adjoint[pl.ds(c, every, stride=pitch), :]
            first = high_part(rows)
            right = jnp.concatenate([first, rows - first], axis=0).astype(BF16)
            both = jnp.dot(left, right, preferred_element_type=F32)
            part = pl.ds(pl.multiple_of(c * width, width), width)
            out[:, part] = chi[:, part] + (both[:levels] + both[levels:])
        put(i).start()

    for i in range(tiles // step):
        put(i).wait()


def exchange(x, axis, size, k):
    return lax.ppermute(x, axis, [(i, i ^ k) for i in range(size)])


def local(chi, bg_std, vert_root, obs_blocks, block_cols, departures, obs_std, obs_target):
    own_tiles, levels, per, width, _ = obs_blocks.shape
    cell_count = chi.shape[1]
    tiles = cell_count // width
    every = vert_root.shape[0]
    slot_rows = departures.shape[0]
    picks = own_tiles * per
    horiz = lax.axis_size("horiz")
    vert = lax.axis_size("vert")
    vert_pos = lax.axis_index("vert").astype(jnp.int32)
    horiz_pos = lax.axis_index("horiz").astype(jnp.int32)
    pitch = tiles + 8
    pos = jnp.stack([vert_pos, horiz_pos * (vert * slot_rows), horiz_pos * tiles])

    slot_shape = (slot_rows // width, width)

    def entries_shape(n):
        return jax.ShapeDtypeStruct((n, 3, *slot_shape), F32)

    cols, entries = call(
        pack_kernel,
        (jax.ShapeDtypeStruct((picks, levels), jnp.int32), entries_shape(1)),
        (
            pos,
            jnp.transpose(block_cols, (0, 2, 1)),
            departures.reshape(slot_shape),
            obs_std.reshape(slot_shape),
            obs_target.reshape(slot_shape),
        ),
        [
            pltpu.VMEM((own_tiles, per, levels), jnp.int32),
            pltpu.VMEM(slot_shape, jnp.int32),
            pltpu.SemaphoreType.DMA((4,)),
        ],
        left=(1, 2, 3, 4),
    )
    received = exchange(entries, "horiz", horiz, 1)
    all_cols = [cols] + [exchange(cols, "vert", vert, k) for k in range(1, vert)]

    part = jax.ShapeDtypeStruct((own_tiles, levels // PARTS, *obs_blocks.shape[2:]), BF16)
    pos, cols, entries = lax.optimization_barrier((pos, cols, entries))
    high, low, bg, *first_blocks = call(
        functools.partial(mix_kernel, levels, pitch),
        (
            jax.ShapeDtypeStruct((every * tiles, width), BF16),
            jax.ShapeDtypeStruct((levels * tiles, width), BF16),
            jax.ShapeDtypeStruct(bg_std.shape, F32),
        )
        + (part,) * IN_MIX,
        (pos, vert_root, chi, bg_std, obs_blocks),
        [
            pltpu.VMEM((every * pitch, width), F32),
            pltpu.VMEM(vert_root.shape, F32),
            pltpu.VMEM(chi.shape, F32),
            pltpu.SemaphoreType.DMA((tiles // MIX_STEP + 1,)),
            pltpu.SemaphoreType.DMA,
            pltpu.SemaphoreType.DMA((IN_MIX * SPLIT,)),
        ],
        left=(1, 2, 3, 4),
        mib=12,
    )
    picked_shape = (levels, picks, width)
    own_picks, joined, *sent_picks = call(
        functools.partial(pick_kernel, vert),
        (jax.ShapeDtypeStruct(picked_shape, F32), entries_shape(2))
        + (jax.ShapeDtypeStruct(picked_shape, BF16),) * (vert - 1)
        + (part,) * IN_PICK,
        (
            pos,
            *all_cols,
            high,
            low,
            entries,
            received,
            obs_blocks,
        ),
        [pltpu.SemaphoreType.DMA((IN_PICK * SPLIT,))],
        left=(5 + vert,),
    )
    second_blocks = sent_picks[vert - 1 :]
    got_picks = [exchange(sent_picks[k - 1], "vert", vert, k) for k in range(1, vert)]
    groups = [joined] + [exchange(joined, "horiz", horiz, k) for k in range(2, horiz, 2)]
    scale, *third_blocks = call(
        functools.partial(scale_kernel, pitch),
        (
            jax.ShapeDtypeStruct(picked_shape, F32),
        )
        + (part,) * IN_SCALE,
        (pos, cols, bg, obs_blocks),
        [pltpu.VMEM((levels * pitch, width), F32), pltpu.SemaphoreType.DMA((IN_SCALE * SPLIT,))],
        left=(3,),
        mib=6,
    )
    blocks = [*first_blocks, *second_blocks, *third_blocks]
    rest = PARTS - len(blocks)
    (placed,) = call(
        functools.partial(place_kernel, own_tiles),
        (jax.ShapeDtypeStruct((2, own_tiles, width), F32),),
        (pos, *groups),
    )
    partial, *last_blocks = call(
        functools.partial(forward_kernel, vert),
        (jax.ShapeDtypeStruct((2, own_tiles, width), F32),) + (part,) * rest,
        (pos, placed, scale, own_picks, *got_picks, *blocks, obs_blocks),
        [
            pltpu.VMEM((picks - VECTOR_TILES * per, width), F32),
            pltpu.VMEM((levels // PARTS, VECTOR_TILES * per, width), F32),
            pltpu.VMEM((VECTOR_TILES, width, width), F32),
            pltpu.SemaphoreType.DMA((rest * SPLIT,)),
        ],
        left=(3 + vert + len(blocks),),
    )
    blocks = [*blocks, *last_blocks]
    partials = [partial] + [exchange(partial, "vert", vert, k) for k in range(1, vert)]
    half_shape = (levels // 2, picks, width)
    sent = []
    for h in range(2):
        weighted, values = call(
            functools.partial(backward_kernel, vert, h),
            (jax.ShapeDtypeStruct(slot_shape, F32), jax.ShapeDtypeStruct(half_shape, BF16)),
            (pos, *partials, scale, *blocks[h * PARTS // 2 : (h + 1) * PARTS // 2]),
            [pltpu.VMEM((picks, width), F32), pltpu.VMEM((vert, *slot_shape), F32)],
        )
        sent.append([values] + [exchange(values, "vert", vert, k) for k in range(1, vert)])
    adjoint_shape = jax.ShapeDtypeStruct((every * pitch, width), F32)
    flipped = pltpu.VMEM((vert, levels, picks), jnp.int32)
    adjoint, mixing = call(
        functools.partial(scatter_kernel, vert, pitch),
        (adjoint_shape, jax.ShapeDtypeStruct((2 * levels, 2 * every), F32)),
        (pos, vert_root, *all_cols, *sent[0], sent[1][0]),
        [pltpu.VMEM((every, every), F32), flipped],
    )
    gradient, _ = call(
        functools.partial(gradient_kernel, vert, pitch),
        (jax.ShapeDtypeStruct(chi.shape, F32), adjoint_shape),
        (pos, mixing, chi, *all_cols, *sent[1][1:], adjoint),
        [
            flipped,
            pltpu.VMEM(chi.shape, F32),
            pltpu.SemaphoreType.DMA((tiles // GRAD_STEP,)),
        ],
        mib=6,
        outside=(0,),
        aliases={2 + 2 * vert: 1},
    )
    return gradient, weighted.reshape(slot_rows)


def solution(mesh):
    in_specs = (
        P("vert", "horiz"),
        P("vert", "horiz"),
        P(),
        P("horiz", "vert", None, None, None),
        P("horiz", "vert", None),
        P(("horiz", "vert")),
        P(("horiz", "vert")),
        P(("horiz", "vert")),
    )
    out_specs = (P("vert", "horiz"), P(("horiz", "vert")))
    return jax.shard_map(local, mesh=mesh, in_specs=in_specs, out_specs=out_specs, check_vma=False)
```
